32 devices in a mesh: row: 4 (over y, x), col: 8 (over z, core).
Axes of the slice: x: 2, y: 2, z: 4, core: 2. Of those that a mesh axis runs over, the one named last changes fastest.
Arguments:
- mode_profiles: bfloat16 [32768, 2048], P(('row', 'col')), may hold values from -0.032958984 to 0.032958984
- region_labels: int32 [32768], P(('row', 'col')), may hold values from 0 to 15
- gain_table: float32 [16], replicated, may hold values from 0.25 to 2
- index_table: float32 [16], replicated, may hold values from -2 to 2
- field_in: bfloat16 [2048, 2048], P('row', 'col'), may hold values from -2 to 2
Outputs:
- field_out: bfloat16 [2048, 2048], P('row', 'col')
The draws below stay inside these ranges and needn't reach their ends.
All inputs are finite; a program needn't handle non-finite values.
Results may differ from the reference program's by a relative error of at most 0.02.
Values may be sent and summed in bfloat16 or wider, within the bound.
A program may use at most 64 MiB of HBM per device.

```python
import math
import jax
import jax.numpy as jnp
from jax import lax

MODES = 2048
REGIONS = 16
TERMS = 6
POINTS = 32768


def touch_ends(result, key, least, largest):
    index_at = [jax.random.randint(jax.random.fold_in(key, axis), (), 0, length) for axis, length in enumerate(result.shape)]
    main_axis = result.shape.index(max(result.shape))
    beside = index_at[:main_axis] + [(index_at[main_axis] + 1) % result.shape[main_axis]] + index_at[main_axis + 1:]
    return result.at[tuple(index_at)].set(least).at[tuple(beside)].set(largest)


def strengthened(result, rng, source, target, shards_of, factor):
    def block_of(axis_at):
        return (jnp.arange(result.shape[axis_at]) // (result.shape[axis_at] // shards_of)).reshape((-1,) + (1,) * (result.ndim - 1 - axis_at))

    near = jax.random.permutation(rng, shards_of)[block_of(target)]
    other_side = (block_of(target) + shards_of // 2) % shards_of
    return jnp.where((block_of(source) == near) | (block_of(source) == other_side), factor * result, result)


def level_of(own_key, shape, cuts, least, largest):
    def one(axis_at, parts):
        heights = jax.random.uniform(jax.random.fold_in(jax.random.fold_in(own_key, 6), axis_at), (parts,), jnp.float32, least / len(cuts), largest / len(cuts))
        return jnp.repeat(jnp.exp(heights), shape[axis_at] // parts).reshape((-1,) + (1,) * (len(shape) - axis_at - 1))

    gain = one(*cuts[0])
    for cut in cuts[1:]:
        gain = gain * one(*cut)
    return gain


def bell_draw(key, dims, width, limit, shards=(), held_as=jnp.bfloat16):
    loudness = level_of(key, dims, shards, -0.22, 0.18) if shards else 1.0
    values = jax.random.normal(key, dims, jnp.float32) * width * loudness
    return jnp.minimum(jnp.maximum(values, -limit), limit).astype(held_as)


def gaussian_with(stream_key, extent, scale, reach, shards, heavy, held_as=jnp.bfloat16):
    values = scale * jax.random.normal(stream_key, extent, jnp.float32)
    if shards:
        values = values * level_of(stream_key, extent, shards, -0.22, 0.18)
    return jnp.clip(strengthened(values, jax.random.fold_in(stream_key, 3), *heavy), -reach, reach).astype(held_as)


def setup_inputs(seed: int = 0) -> dict:
    keys = jax.random.split(jax.random.key(seed), 6)
    return {
        "mode_profiles": gaussian_with(keys[0], (POINTS, MODES), (POINTS ** -0.5), 0.032958984, ((0, 32),), (0, 1, 32, 2.75)),
        "region_labels": touch_ends(jax.random.randint(keys[1], (POINTS,), 0, REGIONS), jax.random.fold_in(keys[1], 1), 0, REGIONS - 1).astype(jnp.int32),
        "gain_table": jnp.clip(jnp.exp(jax.random.uniform(keys[2], (REGIONS,), jnp.float32, math.log(0.25), math.log(2.0))), 0.25, 2.0),
        "index_table": jnp.clip(jax.random.uniform(keys[3], (REGIONS,), jnp.float32, -2.0, 2.0), -2.0, 2.0),
        "field_in": bell_draw(keys[4], (MODES, MODES), 0.3, 2.0, ((0, 4), (1, 8))),
    }


def reference(mode_profiles, region_labels, gain_table, index_table, field_in):
    table = gain_table + index_table
    weight = table[region_labels]
    profiles = mode_profiles.astype(jnp.float32)
    scaled = (profiles * weight[:, None]).astype(jnp.bfloat16)
    coupling = jnp.dot(profiles.T, scaled.astype(jnp.float32), precision=lax.Precision.HIGHEST, preferred_element_type=jnp.float32)
    coupling = coupling.astype(jnp.bfloat16)
    start = field_in.astype(jnp.float32)
    carry = field_in
    for order in range(TERMS, 0, -1):
        product = jnp.dot(coupling, carry, preferred_element_type=jnp.float32)
        carry = (start + (1.0 / order) * product).astype(jnp.bfloat16)
    return carry
```

```python
import functools

import jax
import jax.numpy as jnp
from jax import lax
from jax.experimental import pallas as pl
from jax.experimental.pallas import tpu as pltpu
from jax.sharding import PartitionSpec as P

TERMS = 6
LANES = 128
MESH = pl.DeviceIdType.MESH


def lowest_bit(g):
    t = 0
    while not (g >> t) & 1:
        t += 1
    return t


def kernel(R, Z, n, labels_hbm, gain_ref, index_ref, p_hbm, f_hbm, out_ref, p_ref, labels_ref, f_ref, ft, s2, part, r0, rt, rz, cx, x0, xs, ot, send_sem, recv_sem, z_sem, spread_sem, load_sem, small_sem):
    bits = R.bit_length() - 1
    blocks = n // LANES
    half = blocks // 2
    width = (half + 1) * LANES
    depth = n // (R * Z * 2)
    mine_cols = x0.shape[0]
    row_rows = n // R
    step_rows = min(2 * LANES, row_rows)
    steps = row_rows // step_rows
    per_step = Z // steps
    row, col = lax.axis_index("row"), lax.axis_index("col")
    z, h = col // 2, col % 2
    partner = (row, z * 2 + 1 - h)

    def flip(r, t):
        mask0, mask1 = 1 << t, 1 << (bits - 1 - t)
        mask = mask0 + h * (mask1 - mask0)
        return r + mask * (1 - 2 * ((r // mask) % 2))

    def row_of(g):
        r = row
        for t in range(bits):
            if (g >> t) & 1:
                r = flip(r, t)
        return r

    def mirrored(g):
        return sum(((g >> t) & 1) << (bits - 1 - t) for t in range(bits))

    def low_of(g):
        return lowest_bit(g) if g else bits

    def group_of(p):
        return (z // per_step + 1 + p) % steps

    def z_of(p, e):
        return group_of(p) * per_step + (z % per_step + 1 + e) % per_step

    def near(p):
        if p == 0:
            return z
        edge = jnp.minimum(z, Z - 1 - z)
        away = 1 - 2 * (2 * z // Z)
        both_sides = away * (p // 2) if p % 2 == 0 else -away * ((p + 1) // 2)
        return z + jnp.where(p <= 2 * edge, both_sides, away * (p - edge))

    def strip_of(r, zz, hh):
        return (r * Z + zz) * 2 + hh

    def rows_of(ref, s):
        return ref.at[pl.ds(pl.multiple_of(s * depth, depth), depth), :]

    def window_of(s):
        start = pl.multiple_of((s * depth // LANES) * LANES, LANES)
        return cx.at[pl.ds(pl.multiple_of(s * depth, depth), depth), pl.ds(start, width)]

    ids, started = {}, []

    def slot(key):
        return recv_sem.at[ids.setdefault(key, len(ids))]

    def send_to(src, dst, device, sem):
        copy = pltpu.make_async_remote_copy(
            src_ref=src, dst_ref=dst, send_sem=send_sem.at[len(started)],
            recv_sem=sem, device_id=device, device_id_type=MESH)
        copy.start()
        started.append(copy)

    def send(src, dst, device, key):
        send_to(src, dst, device, slot(key))

    def arrived_at(ref, sem):
        pltpu.make_async_remote_copy(
            src_ref=ref, dst_ref=ref, send_sem=send_sem.at[0],
            recv_sem=sem, device_id=partner, device_id_type=MESH).wait_recv()

    def arrived(ref, key):
        arrived_at(ref, slot(key))

    rows_at_once = LANES
    loads = p_ref.shape[0] // rows_at_once

    def load(i):
        rows = pl.ds(i * rows_at_once, rows_at_once)
        return pltpu.make_async_copy(p_hbm.at[rows, :], p_ref.at[rows, :], load_sem.at[i])

    load_labels = pltpu.make_async_copy(labels_hbm, labels_ref, small_sem.at[0])
    load_field = pltpu.make_async_copy(f_hbm, f_ref, small_sem.at[1])
    load_labels.start()
    load(0).start()
    load_field.start()
    for i in range(1, loads):
        load(i).start()

    barrier = pltpu.get_barrier_semaphore()
    peers = [(row_of(g), col) for g in range(1, R)]
    peers += [(row, ((z + k) % Z) * 2 + h) for k in range(1, Z)] + [partner]
    for peer in peers:
        pl.semaphore_signal(barrier, inc=1, device_id=peer, device_id_type=MESH)

    def columns_at(r):
        return pl.ds(pl.multiple_of(r * row_rows, row_rows), row_rows)

    def slab_at(r):
        return pl.ds(pl.multiple_of(r * mine_cols, mine_cols), mine_cols)

    load_labels.wait()
    labels = labels_ref[...]
    weight = jnp.zeros(labels.shape, jnp.float32)
    for region in range(gain_ref.shape[0]):
        weight = jnp.where(labels == region, gain_ref[region] + index_ref[region], weight)
    for i in range(loads):
        rows = pl.ds(i * rows_at_once, rows_at_once)
        along = jnp.broadcast_to(weight[i : i + 1, :], (LANES, LANES)).T
        load(i).wait()
        for c in range(n // LANES):
            columns = pl.ds(c * LANES, LANES)
            scaled = (p_ref[rows, columns].astype(jnp.float32) * along).astype(jnp.bfloat16)
            s2[rows, columns] = scaled
            if c * LANES < width - LANES:
                s2[rows, pl.ds(n + c * LANES, LANES)] = scaled
        if i == 0:
            load_field.wait()
            ft[...] = f_ref[...].T

    pl.semaphore_wait(barrier, len(peers))
    for g in range(1, R):
        to = row_of(g)
        send(ft.at[slab_at(to), :], x0.at[:, columns_at(row)], (to, col), ("field", g))
    x0[:, columns_at(row)] = ft[slab_at(row), :]

    order = sorted(range(R), key=lambda g: (low_of(g), -g))
    stage_slot = {}
    for t in range(bits):
        for g in range(R):
            if g % (2 << t) == 0:
                stage_slot[t, g] = len(stage_slot)

    def reduce_one(p, g, e):
        low, j = low_of(g), p * per_step + e
        zz = z_of(p, e)
        arrived(r0.at[g * Z + j], ("core", g, j))
        own = rows_of(part, strip_of(row_of(g), zz, h))
        total = own[...].astype(jnp.float32) + r0[g * Z + j].astype(jnp.float32)
        for t in range(low):
            piece = rt.at[stage_slot[t, g] * Z + j]
            arrived(piece, ("row", t, g, j))
            total = total + piece[...].astype(jnp.float32)
        if g:
            own[...] = total.astype(jnp.bfloat16)
            seen = g ^ (1 << low)
            send(own, rt.at[stage_slot[low, seen] * Z + j], (flip(row, low), col), ("row", low, seen, j))
        elif j < Z - 1:
            own[...] = total.astype(jnp.bfloat16)
            send_to(own, rz.at[z], (row, zz * 2 + h), z_sem.at[z])
        else:
            for i in range(1, Z):
                source = (z + i) % Z
                arrived_at(rz.at[source], z_sem.at[source])
                total = total + rz[source].astype(jnp.float32)
            window_of(strip_of(row, z, h))[...] = total.astype(jnp.bfloat16)

    sequence = [(p, g) for p in range(steps) for g in order]
    waiting = []
    for p, g in sequence:
        ready = max(sequence.index((p, g)), sequence.index((p, mirrored(g))))
        waiting += [((p + low_of(g), e, -low_of(g)), ready + 1 + 3 * low_of(g), p, g, e) for e in range(per_step)]
    for at, (p, g) in enumerate(sequence):
        r, q = row_of(g), group_of(p)
        base = pl.multiple_of(r * row_rows + q * step_rows, step_rows)
        left = p_ref[:, pl.ds(base, step_rows)].T
        spread_width = width + step_rows - LANES
        both = jnp.dot(left, s2[:, pl.ds(base, spread_width)], preferred_element_type=jnp.float32)
        for k in range(step_rows // LANES):
            part[pl.ds(base + k * LANES, LANES), :] = both[k * LANES : (k + 1) * LANES, k * LANES : k * LANES + width].astype(jnp.bfloat16)
        for e in range(per_step):
            j = p * per_step + e
            send(rows_of(part, strip_of(r, z_of(p, e), 1 - h)), r0.at[mirrored(g) * Z + j], partner, ("core", mirrored(g), j))
        due = [item for item in waiting if item[1] <= at]
        waiting = [item for item in waiting if item[1] > at]
        for _, _, p1, g1, e1 in due:
            reduce_one(p1, g1, e1)
    for _, _, p, g, e in sorted(waiting):
        reduce_one(p, g, e)

    def spread(g, strip, p):
        view = window_of(strip)
        for t in reversed(range(low_of(g))):
            send(view, view, (flip(row, t), col), ("spread", g | (1 << t), p))
        send(view, view, partner, ("spread_core", mirrored(g), p))

    def mirror_block(i):
        rows = pl.ds(pl.multiple_of(i * LANES, LANES), LANES)
        for d in range(1, half):
            to = pl.multiple_of(((i + d) % blocks) * LANES, LANES)
            block = cx[rows, pl.ds(pl.multiple_of((i + d) * LANES, LANES), LANES)]
            cx[pl.ds(to, LANES), rows] = block.T

    def forward(g, p):
        strip = strip_of(row_of(g), near(p), h)
        if g:
            arrived(window_of(strip), ("spread", g, p))
        elif p:
            arrived_at(window_of(strip), spread_sem.at[near(p)])
        spread(g, strip, p)

    def whole_block(g, p):
        arrived(window_of(strip_of(row_of(g), near(p), 1 - h)), ("spread_core", g, p))
        if 2 * depth == LANES:
            mirror_block(row_of(g) * Z + near(p))

    mine = window_of(strip_of(row, z, h))
    for p in range(1, Z):
        send_to(mine, mine, (row, near(p) * 2 + h), spread_sem.at[z])

    def tick(item):
        g, p = item
        count = bin(g).count("1")
        return p + count + (0.3 - 0.1 * count if low_of(g) == 0 else 0.05)

    schedule = sorted(((g, p) for g in range(R) for p in range(Z)), key=tick)
    blocks_left = sorted((max(schedule.index((g, p)), schedule.index((mirrored(g), p))), g, p) for g, p in schedule)
    for at, (g, p) in enumerate(schedule):
        last = at == len(schedule) - 1
        while blocks_left and last and blocks_left[0][0] < at:
            whole_block(*blocks_left.pop(0)[1:])
        forward(g, p)
        while blocks_left and (blocks_left[0][0] + 2 <= at or at == 0 and blocks_left[0][0] == 0):
            whole_block(*blocks_left.pop(0)[1:])
    for _, g, p in blocks_left:
        whole_block(g, p)
    if 2 * depth != LANES:
        pl.loop(0, blocks)(mirror_block)

    for i in range(half, blocks):
        rows = pl.ds(i * LANES, LANES)
        over = (i + half + 1 - blocks) * LANES
        cx[rows, :over] = cx[rows, n : n + over]

    for g in range(1, R):
        arrived(x0.at[:, columns_at(row_of(g))], ("field", g))
    for index in range(TERMS - 1):
        source = x0 if index == 0 else xs.at[(index + 1) % 2]
        target = xs.at[index % 2]
        scale = 1.0 / (TERMS - index)

        product = jnp.dot(source[...], cx[:, :n], preferred_element_type=jnp.float32)
        target[...] = (x0[...].astype(jnp.float32) + scale * product).astype(jnp.bfloat16)

    source, last = xs.at[TERMS % 2], xs.at[(TERMS - 1) % 2]
    for g in reversed(range(R)):
        to = row_of(g)
        product = jnp.dot(source[...], cx[:, columns_at(to)], preferred_element_type=jnp.float32)
        value = (x0[:, columns_at(to)].astype(jnp.float32) + product).astype(jnp.bfloat16)
        if g:
            last[:, columns_at(to)] = value
            send(last.at[:, columns_at(to)], ot.at[slab_at(row), :], (to, col), ("out", g))
        else:
            out_ref[slab_at(row), :] = value
    for g in reversed(range(1, R)):
        source = slab_at(row_of(g))
        arrived(ot.at[source, :], ("out", g))
        out_ref[source, :] = ot[source, :]
    for copy in started:
        copy.wait_send()


def on_device(R, Z, mode_profiles, region_labels, gain_table, index_table, field_in):
    points, n = mode_profiles.shape
    width = n // 2 + LANES
    depth = n // (R * Z * 2)
    mine_cols = field_in.shape[1] // R
    messages = 2 * R * Z + 2 * (R - 1) * Z + 2 * (Z - 1) + 2 * (R - 1)
    bf16 = jnp.bfloat16
    turned = pl.pallas_call(
        functools.partial(kernel, R, Z, n),
        out_shape=jax.ShapeDtypeStruct(field_in.shape[::-1], bf16),
        in_specs=[
            pl.BlockSpec(memory_space=pl.ANY),
            pl.BlockSpec(memory_space=pltpu.SMEM),
            pl.BlockSpec(memory_space=pltpu.SMEM),
            pl.BlockSpec(memory_space=pl.ANY),
            pl.BlockSpec(memory_space=pl.ANY),
        ],
        out_specs=pl.BlockSpec(memory_space=pltpu.VMEM),
        scratch_shapes=[
            pltpu.VMEM((points, n), bf16),
            pltpu.VMEM((points // LANES, LANES), jnp.int32),
            pltpu.VMEM(field_in.shape, bf16),
            pltpu.VMEM(field_in.shape[::-1], bf16),
            pltpu.VMEM((points, n + width - LANES), bf16),
            pltpu.VMEM((n, width), bf16),
            pltpu.VMEM((R * Z, depth, width), bf16),
            pltpu.VMEM(((R - 1) * Z, depth, width), bf16),
            pltpu.VMEM((Z, depth, width), bf16),
            pltpu.VMEM((n, n + width - LANES), bf16),
            pltpu.VMEM((mine_cols, n), bf16),
            pltpu.VMEM((2, mine_cols, n), bf16),
            pltpu.VMEM(field_in.shape[::-1], bf16),
            pltpu.SemaphoreType.DMA((messages,)),
            pltpu.SemaphoreType.DMA((messages,)),
            pltpu.SemaphoreType.DMA((Z,)),
            pltpu.SemaphoreType.DMA((Z,)),
            pltpu.SemaphoreType.DMA((points // LANES,)),
            pltpu.SemaphoreType.DMA((2,)),
        ],
        compiler_params=pltpu.CompilerParams(
            collective_id=0, has_side_effects=True, vmem_limit_bytes=60 * 1024 * 1024),
    )(region_labels.reshape(-1, LANES), gain_table, index_table, mode_profiles, field_in)
    return turned.T


def solution(mesh):
    return jax.shard_map(
        functools.partial(on_device, mesh.shape["row"], mesh.shape["col"] // 2),
        mesh=mesh,
        in_specs=(P(("row", "col"), None), P(("row", "col")), P(), P(), P("row", "col")),
        out_specs=P("row", "col"),
        check_vma=False,
    )
```

```python
import functools

import jax
import jax.numpy as jnp
from jax import lax
from jax.experimental import pallas as pl
from jax.experimental.pallas import tpu as pltpu
from jax.sharding import PartitionSpec as P

TERMS = 6
LANES = 128
MESH = pl.DeviceIdType.MESH


def lowest_bit(g):
    t = 0
    while not (g >> t) & 1:
        t += 1
    return t


SPLITS = 3
LINK, ROUTED, NEAR = 88e3, 2.2, 1.1


def cuts_of(width):
    tiles = width // LANES
    edges = [-(-tiles * c // SPLITS) * LANES for c in range(SPLITS + 1)]
    return [(first, after - first) for first, after in zip(edges, edges[1:])]


def planned(R, Z, steps, order, mirrored, low_of, depth, cuts):
    per_step = Z // steps
    final = (steps - 1, 0, per_step - 1)
    ops = []
    for c in range(len(cuts)):
        ops += [("product", c, p, g) for p in range(steps) for g in order]
        ops += [("reduce", c, p, g, e) for p in range(steps) for g in order for e in range(per_step)]
        ops += [("forward", c, g, p) for p in range(Z) for g in range(R)]
        ops += [("block", c, g, p) for p in range(Z) for g in range(R)]
    at, free = {}, {"row": 4.0, "z": 4.0, "core": 4.0}

    def needs(op):
        kind, c = op[:2]
        if kind == "product":
            return []
        if kind == "reduce":
            p, g, e = op[2:]
            j = p * per_step + e
            keys = [("product", c, p, g), ("core", c, g, j)] + [("row", c, t, g, j) for t in range(low_of(g))]
            return keys + ([("sums", c, i) for i in range(Z - 1)] if (p, g, e) == final else [])
        g, p = op[2:]
        if kind == "block":
            return [("forward", c, g, p), ("spread_core", c, g, p)]
        return [("spread", c, g, p) if (g or p) else ("reduce", c, *final)]

    def rank(op):
        kind, c = op[:2]
        if kind == "reduce":
            p, g, e = op[2:]
            return (1, c, p, low_of(g), -g, e)
        if kind == "forward":
            return (0, c, op[3], -low_of(op[2]))
        return (2 if kind == "product" else 3, c)

    def sent(now, link, amount, key):
        free[link] = max(free[link], now) + amount
        at[key] = free[link] + (NEAR if link == "core" else ROUTED)

    now, left, done = 4.4, list(ops), []
    while left:
        able = []
        for op in left:
            keys = needs(op)
            if all(key in at for key in keys):
                able.append((max([at[key] for key in keys], default=0.0), op))
        ripe = [item for item in able if item[0] <= now]
        if ripe:
            start, op = min(ripe, key=lambda item: rank(item[1]))
        else:
            start, op = min(able, key=lambda item: (item[0], rank(item[1])))
        now = max(now, start)
        left.remove(op)
        done.append(op)
        kind, c = op[:2]
        strip = depth * cuts[c][1] * 2 / LINK
        if kind == "product":
            p, g = op[2:]
            now += cuts[c][1] / LANES * 0.11 + 0.1
            for e in range(per_step):
                sent(now, "core", strip / 7, ("core", c, mirrored(g), p * per_step + e))
        elif kind == "reduce":
            p, g, e = op[2:]
            now += 0.1
            if g:
                low = low_of(g)
                sent(now, "row", strip, ("row", c, low, g ^ (1 << low), p * per_step + e))
            elif (p, g, e) != final:
                sent(now, "z", strip * 8 / 3, ("sums", c, p * per_step + e))
        elif kind == "forward":
            g, p = op[2:]
            now += 0.1
            if g == 0 and p == 0:
                for k in range(1, Z):
                    sent(now, "z", strip * 8 / 3, ("spread", c, 0, k))
            for there in reached_from(g, p, c == len(cuts) - 1 and p == Z - 1, R, low_of):
                sent(now, "row", strip, ("spread", c, there, p))
            sent(now, "core", strip / 7, ("spread_core", c, mirrored(g), p))
        else:
            now += cuts[c][1] / LANES * 0.06
        at[op] = now
    return done


def reached_from(g, p, direct, R, low_of):
    if direct:
        return list(reversed(range(1, R))) if g == 0 else []
    return [g | (1 << t) for t in reversed(range(low_of(g)))]


def kernel(R, Z, n, labels_ref, gain_ref, index_ref, p_hbm, f_hbm, out_ref, p_ref, f_ref, ft, s2, part, r0, rt, rz, cx, x0, xs, ot, send_sem, recv_sem, z_sem, spread_sem, load_sem, small_sem):
    bits = R.bit_length() - 1
    blocks = n // LANES
    half = blocks // 2
    width = (half + 1) * LANES
    depth = n // (R * Z * 2)
    mine_cols = x0.shape[0]
    row_rows = n // R
    step_rows = min(2 * LANES, row_rows)
    steps = row_rows // step_rows
    per_step = Z // steps
    row, col = lax.axis_index("row"), lax.axis_index("col")
    z, h = col // 2, col % 2
    partner = (row, z * 2 + 1 - h)

    def flip(r, t):
        mask0, mask1 = 1 << t, 1 << (bits - 1 - t)
        mask = mask0 + h * (mask1 - mask0)
        return r + mask * (1 - 2 * ((r // mask) % 2))

    def row_of(g):
        r = row
        for t in range(bits):
            if (g >> t) & 1:
                r = flip(r, t)
        return r

    def mirrored(g):
        return sum(((g >> t) & 1) << (bits - 1 - t) for t in range(bits))

    def low_of(g):
        return lowest_bit(g) if g else bits

    def group_of(p):
        return (z // per_step + 1 + p) % steps

    def z_of(p, e):
        return group_of(p) * per_step + (z % per_step + 1 + e) % per_step

    def near(p):
        if p == 0:
            return z
        edge = jnp.minimum(z, Z - 1 - z)
        away = 1 - 2 * (2 * z // Z)
        both_sides = away * (p // 2) if p % 2 == 0 else -away * ((p + 1) // 2)
        return z + jnp.where(p <= 2 * edge, both_sides, away * (p - edge))

    def strip_of(r, zz, hh):
        return (r * Z + zz) * 2 + hh

    cuts = cuts_of(width)

    def columns_of(c):
        return pl.ds(*cuts[c])

    def rows_of(ref, s, c):
        return ref.at[pl.ds(pl.multiple_of(s * depth, depth), depth), columns_of(c)]

    def window_of(s, c):
        first, size = cuts[c]
        start = pl.multiple_of((s * depth // LANES) * LANES + first, LANES)
        return cx.at[pl.ds(pl.multiple_of(s * depth, depth), depth), pl.ds(start, size)]

    ids, started = {}, []

    def slot(key):
        return recv_sem.at[ids.setdefault(key, len(ids))]

    def send_to(src, dst, device, sem):
        copy = pltpu.make_async_remote_copy(
            src_ref=src, dst_ref=dst, send_sem=send_sem.at[len(started)],
            recv_sem=sem, device_id=device, device_id_type=MESH)
        copy.start()
        started.append(copy)

    def send(src, dst, device, key):
        send_to(src, dst, device, slot(key))

    def arrived_at(ref, sem):
        pltpu.make_async_remote_copy(
            src_ref=ref, dst_ref=ref, send_sem=send_sem.at[0],
            recv_sem=sem, device_id=partner, device_id_type=MESH).wait_recv()

    def arrived(ref, key):
        arrived_at(ref, slot(key))

    rows_at_once = LANES
    loads = p_ref.shape[0] // rows_at_once

    def load(i):
        rows = pl.ds(i * rows_at_once, rows_at_once)
        return pltpu.make_async_copy(p_hbm.at[rows, :], p_ref.at[rows, :], load_sem.at[i])

    load_field = pltpu.make_async_copy(f_hbm, f_ref, small_sem.at[0])
    load(0).start()
    load_field.start()
    for i in range(1, loads):
        load(i).start()

    barrier = pltpu.get_barrier_semaphore()
    peers = [(row_of(g), col) for g in range(1, R)]
    peers += [(row, ((z + k) % Z) * 2 + h) for k in range(1, Z)] + [partner]
    for peer in peers:
        pl.semaphore_signal(barrier, inc=1, device_id=peer, device_id_type=MESH)

    def columns_at(r):
        return pl.ds(pl.multiple_of(r * row_rows, row_rows), row_rows)

    def slab_at(r):
        return pl.ds(pl.multiple_of(r * mine_cols, mine_cols), mine_cols)

    labels = labels_ref[...]
    weight = jnp.zeros(labels.shape, jnp.float32)
    for region in range(gain_ref.shape[0]):
        weight = jnp.where(labels == region, gain_ref[region] + index_ref[region], weight)
    for i in range(loads):
        rows = pl.ds(i * rows_at_once, rows_at_once)
        along = jnp.broadcast_to(weight[i : i + 1, :], (LANES, LANES)).T
        load(i).wait()
        for c in range(n // LANES):
            columns = pl.ds(c * LANES, LANES)
            scaled = (p_ref[rows, columns].astype(jnp.float32) * along).astype(jnp.bfloat16)
            s2[rows, columns] = scaled
            if c * LANES < width - LANES:
                s2[rows, pl.ds(n + c * LANES, LANES)] = scaled
        if i == loads // 2:
            load_field.wait()
            ft[...] = f_ref[...].T

    pl.semaphore_wait(barrier, len(peers))
    for g in range(1, R):
        to = row_of(g)
        send(ft.at[slab_at(to), :], x0.at[:, columns_at(row)], (to, col), ("field", g))
    x0[:, columns_at(row)] = ft[slab_at(row), :]

    order = sorted(range(R), key=lambda g: (low_of(g), -g))
    stage_slot = {}
    for t in range(bits):
        for g in range(R):
            if g % (2 << t) == 0:
                stage_slot[t, g] = len(stage_slot)

    def reduce(c, p, g, e):
        low, j = low_of(g), p * per_step + e
        zz, columns = z_of(p, e), columns_of(c)
        arrived(r0.at[g * Z + j, :, columns], ("core", c, g, j))
        own = rows_of(part, strip_of(row_of(g), zz, h), c)
        total = own[...].astype(jnp.float32) + r0[g * Z + j, :, columns].astype(jnp.float32)
        for t in range(low):
            piece = rt.at[stage_slot[t, g] * Z + j, :, columns]
            arrived(piece, ("row", c, t, g, j))
            total = total + piece[...].astype(jnp.float32)
        if g:
            own[...] = total.astype(jnp.bfloat16)
            seen = g ^ (1 << low)
            send(own, rt.at[stage_slot[low, seen] * Z + j, :, columns], (flip(row, low), col), ("row", c, low, seen, j))
        elif j < Z - 1:
            own[...] = total.astype(jnp.bfloat16)
            send_to(own, rz.at[z, :, columns], (row, zz * 2 + h), z_sem.at[c * Z + z])
        else:
            for i in range(1, Z):
                source = (z + i) % Z
                arrived_at(rz.at[source, :, columns], z_sem.at[c * Z + source])
                total = total + rz[source, :, columns].astype(jnp.float32)
            window_of(strip_of(row, z, h), c)[...] = total.astype(jnp.bfloat16)

    def product(c, p, g):
        first, size = cuts[c]
        r, q = row_of(g), group_of(p)
        base = pl.multiple_of(r * row_rows + q * step_rows, step_rows)
        left = p_ref[:, pl.ds(base, step_rows)].T
        right = s2[:, pl.ds(pl.multiple_of(base + first, LANES), size + step_rows - LANES)]
        both = jnp.dot(left, right, preferred_element_type=jnp.float32)
        for k in range(step_rows // LANES):
            piece = both[k * LANES : (k + 1) * LANES, k * LANES : k * LANES + size]
            part[pl.ds(base + k * LANES, LANES), columns_of(c)] = piece.astype(jnp.bfloat16)
        for e in range(per_step):
            j = p * per_step + e
            there = r0.at[mirrored(g) * Z + j, :, columns_of(c)]
            send(rows_of(part, strip_of(r, z_of(p, e), 1 - h), c), there, partner, ("core", c, mirrored(g), j))

    def mirror_block(i, c):
        rows = pl.ds(pl.multiple_of(i * LANES, LANES), LANES)
        first, size = cuts[c]
        for d in range(max(1, first // LANES), min(half, (first + size) // LANES)):
            to = pl.multiple_of(((i + d) % blocks) * LANES, LANES)
            block = cx[rows, pl.ds(pl.multiple_of((i + d) * LANES, LANES), LANES)]
            cx[pl.ds(to, LANES), rows] = block.T

    def forward(c, g, p):
        view = window_of(strip_of(row_of(g), near(p), h), c)
        if g:
            arrived(view, ("spread", c, g, p))
        elif p:
            arrived_at(view, spread_sem.at[c * Z + near(p)])
        else:
            for k in range(1, Z):
                send_to(view, view, (row, near(k) * 2 + h), spread_sem.at[c * Z + z])
        for there in reached_from(g, p, c == len(cuts) - 1 and p == Z - 1, R, low_of):
            send(view, view, (row_of(there - g), col), ("spread", c, there, p))
        send(view, view, partner, ("spread_core", c, mirrored(g), p))

    def block(c, g, p):
        arrived(window_of(strip_of(row_of(g), near(p), 1 - h), c), ("spread_core", c, g, p))
        if 2 * depth == LANES:
            mirror_block(row_of(g) * Z + near(p), c)

    steps_of = {"product": product, "reduce": reduce, "forward": forward, "block": block}
    for op in planned(R, Z, steps, order, mirrored, low_of, depth, cuts):
        steps_of[op[0]](*op[1:])
    if 2 * depth != LANES:
        @pl.loop(0, blocks)
        def _(i):
            for c in range(len(cuts)):
                mirror_block(i, c)

    for i in range(half, blocks):
        rows = pl.ds(i * LANES, LANES)
        over = (i + half + 1 - blocks) * LANES
        cx[rows, :over] = cx[rows, n : n + over]

    for g in range(1, R):
        arrived(x0.at[:, columns_at(row_of(g))], ("field", g))
    for index in range(TERMS - 1):
        source = x0 if index == 0 else xs.at[(index + 1) % 2]
        target = xs.at[index % 2]
        scale = 1.0 / (TERMS - index)

        product = jnp.dot(source[...], cx[:, :n], preferred_element_type=jnp.float32)
        target[...] = (x0[...].astype(jnp.float32) + scale * product).astype(jnp.bfloat16)

    source, last = xs.at[TERMS % 2], xs.at[(TERMS - 1) % 2]
    for g in reversed(range(R)):
        to = row_of(g)
        product = jnp.dot(source[...], cx[:, columns_at(to)], preferred_element_type=jnp.float32)
        value = (x0[:, columns_at(to)].astype(jnp.float32) + product).astype(jnp.bfloat16)
        if g:
            last[:, columns_at(to)] = value
            send(last.at[:, columns_at(to)], ot.at[slab_at(row), :], (to, col), ("out", g))
        else:
            out_ref[slab_at(row), :] = value
    for g in reversed(range(1, R)):
        source = slab_at(row_of(g))
        arrived(ot.at[source, :], ("out", g))
        out_ref[source, :] = ot[source, :]
    for copy in started:
        copy.wait_send()


def on_device(R, Z, mode_profiles, region_labels, gain_table, index_table, field_in):
    points, n = mode_profiles.shape
    width = n // 2 + LANES
    depth = n // (R * Z * 2)
    mine_cols = field_in.shape[1] // R
    messages = SPLITS * (2 * R * Z + 2 * (R - 1) * Z + 2 * (Z - 1)) + 2 * (R - 1)
    bf16 = jnp.bfloat16
    turned = pl.pallas_call(
        functools.partial(kernel, R, Z, n),
        out_shape=jax.ShapeDtypeStruct(field_in.shape[::-1], bf16),
        in_specs=[
            pl.BlockSpec(memory_space=pltpu.VMEM),
            pl.BlockSpec(memory_space=pltpu.SMEM),
            pl.BlockSpec(memory_space=pltpu.SMEM),
            pl.BlockSpec(memory_space=pl.ANY),
            pl.BlockSpec(memory_space=pl.ANY),
        ],
        out_specs=pl.BlockSpec(memory_space=pltpu.VMEM),
        scratch_shapes=[
            pltpu.VMEM((points, n), bf16),
            pltpu.VMEM(field_in.shape, bf16),
            pltpu.VMEM(field_in.shape[::-1], bf16),
            pltpu.VMEM((points, n + width - LANES), bf16),
            pltpu.VMEM((n, width), bf16),
            pltpu.VMEM((R * Z, depth, width), bf16),
            pltpu.VMEM(((R - 1) * Z, depth, width), bf16),
            pltpu.VMEM((Z, depth, width), bf16),
            pltpu.VMEM((n, n + width - LANES), bf16),
            pltpu.VMEM((mine_cols, n), bf16),
            pltpu.VMEM((2, mine_cols, n), bf16),
            pltpu.VMEM(field_in.shape[::-1], bf16),
            pltpu.SemaphoreType.DMA((messages,)),
            pltpu.SemaphoreType.DMA((messages,)),
            pltpu.SemaphoreType.DMA((SPLITS * Z,)),
            pltpu.SemaphoreType.DMA((SPLITS * Z,)),
            pltpu.SemaphoreType.DMA((points // LANES,)),
            pltpu.SemaphoreType.DMA((1,)),
        ],
        compiler_params=pltpu.CompilerParams(
            collective_id=0, has_side_effects=True, vmem_limit_bytes=60 * 1024 * 1024),
    )(region_labels.reshape(-1, LANES), gain_table, index_table, mode_profiles, field_in)
    return turned.T


def solution(mesh):
    return jax.shard_map(
        functools.partial(on_device, mesh.shape["row"], mesh.shape["col"] // 2),
        mesh=mesh,
        in_specs=(P(("row", "col"), None), P(("row", "col")), P(), P(), P("row", "col")),
        out_specs=P("row", "col"),
        check_vma=False,
    )
```

```python
import functools

import jax
import jax.numpy as jnp
from jax import lax
from jax.experimental import pallas as pl
from jax.experimental.pallas import tpu as pltpu
from jax.sharding import PartitionSpec as P

TERMS = 6
LANES = 128
MESH = pl.DeviceIdType.MESH


def lowest_bit(g):
    t = 0
    while not (g >> t) & 1:
        t += 1
    return t


SPLITS = 3
LINK, ROUTED, NEAR = 88e3, 2.2, 1.1


def cuts_of(width):
    tiles = width // LANES
    edges = [-(-tiles * c // SPLITS) * LANES for c in range(SPLITS + 1)]
    return [(first, after - first) for first, after in zip(edges, edges[1:])]


def planned(R, Z, steps, order, mirrored, low_of, depth, cuts):
    per_step = Z // steps
    final = (steps - 1, 0, per_step - 1)
    ops = []
    for c in range(len(cuts)):
        ops += [("product", c, p, g) for p in range(steps) for g in order]
        ops += [("reduce", c, p, g, e) for p in range(steps) for g in order for e in range(per_step)]
        ops += [("forward", c, g, p) for p in range(Z) for g in range(R)]
        ops += [("block", c, g, p) for p in range(Z) for g in range(R)]
    at, free = {}, {"row": 4.0, "z": 4.0, "core": 4.0}

    def needs(op):
        kind, c = op[:2]
        if kind == "product":
            return []
        if kind == "reduce":
            p, g, e = op[2:]
            j = p * per_step + e
            keys = [("product", c, p, g), ("core", c, g, j)] + [("row", c, t, g, j) for t in range(low_of(g))]
            return keys + ([("sums", c, i) for i in range(Z - 1)] if (p, g, e) == final else [])
        g, p = op[2:]
        if kind == "block":
            return [("forward", c, g, p), ("spread_core", c, g, p)]
        return [("spread", c, g, p) if (g or p) else ("reduce", c, *final)]

    def rank(op):
        kind, c = op[:2]
        if kind == "reduce":
            p, g, e = op[2:]
            return (1, c, p, low_of(g), -g, e)
        if kind == "forward":
            return (0, c, op[3], -low_of(op[2]))
        return (2 if kind == "product" else 3, c)

    def sent(now, link, amount, key):
        free[link] = max(free[link], now) + amount
        at[key] = free[link] + (NEAR if link == "core" else ROUTED)

    now, left, done = 4.4, list(ops), []
    while left:
        able = []
        for op in left:
            keys = needs(op)
            if all(key in at for key in keys):
                able.append((max([at[key] for key in keys], default=0.0), op))
        ripe = [item for item in able if item[0] <= now]
        if ripe:
            start, op = min(ripe, key=lambda item: rank(item[1]))
        else:
            start, op = min(able, key=lambda item: (item[0], rank(item[1])))
        now = max(now, start)
        left.remove(op)
        done.append(op)
        kind, c = op[:2]
        strip = depth * cuts[c][1] * 2 / LINK
        if kind == "product":
            p, g = op[2:]
            now += cuts[c][1] / LANES * 0.11 + 0.1
            for e in range(per_step):
                sent(now, "core", strip / 7, ("core", c, mirrored(g), p * per_step + e))
        elif kind == "reduce":
            p, g, e = op[2:]
            now += 0.1
            if g:
                low = low_of(g)
                sent(now, "row", strip, ("row", c, low, g ^ (1 << low), p * per_step + e))
            elif (p, g, e) != final:
                sent(now, "z", strip * 8 / 3, ("sums", c, p * per_step + e))
        elif kind == "forward":
            g, p = op[2:]
            now += 0.1
            if g == 0 and p == 0:
                for k in range(1, Z):
                    sent(now, "z", strip * 8 / 3, ("spread", c, 0, k))
            for there in reached_from(g, p, c == len(cuts) - 1 and p == Z - 1, R, low_of):
                sent(now, "row", strip, ("spread", c, there, p))
            sent(now, "core", strip / 7, ("spread_core", c, mirrored(g), p))
        else:
            now += cuts[c][1] / LANES * 0.06
        at[op] = now
    return done


def reached_from(g, p, direct, R, low_of):
    if direct:
        return list(reversed(range(1, R))) if g == 0 else []
    return [g | (1 << t) for t in reversed(range(low_of(g)))]


def kernel(R, Z, n, labels_ref, gain_ref, index_ref, p_hbm, f_hbm, out_ref, p_ref, f_ref, ft, s2, part, r0, rt, rz, cx, x0, xs, ot, send_sem, recv_sem, z_sem, spread_sem, load_sem, small_sem):
    bits = R.bit_length() - 1
    blocks = n // LANES
    half = blocks // 2
    width = (half + 1) * LANES
    depth = n // (R * Z * 2)
    mine_cols = x0.shape[0]
    row_rows = n // R
    step_rows = min(2 * LANES, row_rows)
    steps = row_rows // step_rows
    per_step = Z // steps
    row, col = lax.axis_index("row"), lax.axis_index("col")
    z, h = col // 2, col % 2
    partner = (row, z * 2 + 1 - h)

    def flip(r, t):
        mask0, mask1 = 1 << t, 1 << (bits - 1 - t)
        mask = mask0 + h * (mask1 - mask0)
        return r + mask * (1 - 2 * ((r // mask) % 2))

    def row_of(g):
        r = row
        for t in range(bits):
            if (g >> t) & 1:
                r = flip(r, t)
        return r

    def mirrored(g):
        return sum(((g >> t) & 1) << (bits - 1 - t) for t in range(bits))

    def low_of(g):
        return lowest_bit(g) if g else bits

    def group_of(p):
        return (z // per_step + 1 + p) % steps

    def z_of(p, e):
        return group_of(p) * per_step + (z % per_step + 1 + e) % per_step

    def near(p):
        if p == 0:
            return z
        edge = jnp.minimum(z, Z - 1 - z)
        away = 1 - 2 * (2 * z // Z)
        both_sides = away * (p // 2) if p % 2 == 0 else -away * ((p + 1) // 2)
        return z + jnp.where(p <= 2 * edge, both_sides, away * (p - edge))

    def strip_of(r, zz, hh):
        return (r * Z + zz) * 2 + hh

    cuts = cuts_of(width)

    def columns_of(c):
        return pl.ds(*cuts[c])

    def rows_of(ref, s, c):
        return ref.at[pl.ds(pl.multiple_of(s * depth, depth), depth), columns_of(c)]

    def window_of(s, c):
        first, size = cuts[c]
        start = pl.multiple_of((s * depth // LANES) * LANES + first, LANES)
        return cx.at[pl.ds(pl.multiple_of(s * depth, depth), depth), pl.ds(start, size)]

    ids, sends = {}, {}

    def slot(key):
        return recv_sem.at[ids.setdefault(key, len(ids))]

    def send_to(src, dst, device, sem, kind):
        index, copies = sends.get(kind, (len(sends), 0))
        sends[kind] = index, copies + 1
        pltpu.make_async_remote_copy(
            src_ref=src, dst_ref=dst, send_sem=send_sem.at[index],
            recv_sem=sem, device_id=device, device_id_type=MESH).start()

    def send(src, dst, device, key, kind):
        send_to(src, dst, device, slot(key), kind)

    def arrived_at(ref, sem):
        pltpu.make_async_remote_copy(
            src_ref=ref, dst_ref=ref, send_sem=send_sem.at[0],
            recv_sem=sem, device_id=partner, device_id_type=MESH).wait_recv()

    def arrived(ref, key):
        arrived_at(ref, slot(key))

    rows_at_once = LANES
    loads = p_ref.shape[0] // rows_at_once

    def load(i):
        rows = pl.ds(i * rows_at_once, rows_at_once)
        return pltpu.make_async_copy(p_hbm.at[rows, :], p_ref.at[rows, :], load_sem.at[i])

    load_field = pltpu.make_async_copy(f_hbm, f_ref, small_sem.at[0])
    load(0).start()
    load_field.start()
    for i in range(1, loads):
        load(i).start()

    barrier = pltpu.get_barrier_semaphore()
    peers = [(row_of(g), col) for g in range(1, R)]
    peers += [(row, ((z + k) % Z) * 2 + h) for k in range(1, Z)] + [partner]
    for peer in peers:
        pl.semaphore_signal(barrier, inc=1, device_id=peer, device_id_type=MESH)

    def columns_at(r):
        return pl.ds(pl.multiple_of(r * row_rows, row_rows), row_rows)

    def slab_at(r):
        return pl.ds(pl.multiple_of(r * mine_cols, mine_cols), mine_cols)

    labels = labels_ref[...]
    weight = jnp.zeros(labels.shape, jnp.float32)
    for region in range(gain_ref.shape[0]):
        weight = jnp.where(labels == region, gain_ref[region] + index_ref[region], weight)
    for i in range(loads):
        rows = pl.ds(i * rows_at_once, rows_at_once)
        along = jnp.broadcast_to(weight[i : i + 1, :], (LANES, LANES)).T
        load(i).wait()
        for c in range(n // LANES):
            columns = pl.ds(c * LANES, LANES)
            scaled = (p_ref[rows, columns].astype(jnp.float32) * along).astype(jnp.bfloat16)
            s2[rows, columns] = scaled
            if c * LANES < width - LANES:
                s2[rows, pl.ds(n + c * LANES, LANES)] = scaled
        if i == loads // 2:
            load_field.wait()
            ft[...] = f_ref[...].T

    pl.semaphore_wait(barrier, len(peers))
    for g in range(1, R):
        to = row_of(g)
        send(ft.at[slab_at(to), :], x0.at[:, columns_at(row)], (to, col), ("field", g), "field")
    x0[:, columns_at(row)] = ft[slab_at(row), :]

    order = sorted(range(R), key=lambda g: (low_of(g), -g))
    stage_slot = {}
    for t in range(bits):
        for g in range(R):
            if g % (2 << t) == 0:
                stage_slot[t, g] = len(stage_slot)

    def reduce(c, p, g, e):
        low, j = low_of(g), p * per_step + e
        zz, columns = z_of(p, e), columns_of(c)
        arrived(r0.at[g * Z + j, :, columns], ("core", c, g, j))
        own = rows_of(part, strip_of(row_of(g), zz, h), c)
        total = own[...].astype(jnp.float32) + r0[g * Z + j, :, columns].astype(jnp.float32)
        for t in range(low):
            piece = rt.at[stage_slot[t, g] * Z + j, :, columns]
            arrived(piece, ("row", c, t, g, j))
            total = total + piece[...].astype(jnp.float32)
        if g:
            own[...] = total.astype(jnp.bfloat16)
            seen = g ^ (1 << low)
            send(own, rt.at[stage_slot[low, seen] * Z + j, :, columns], (flip(row, low), col), ("row", c, low, seen, j), ("sum", c))
        elif j < Z - 1:
            own[...] = total.astype(jnp.bfloat16)
            send_to(own, rz.at[z, :, columns], (row, zz * 2 + h), z_sem.at[c * Z + z], ("sum", c))
        else:
            for i in range(1, Z):
                source = (z + i) % Z
                arrived_at(rz.at[source, :, columns], z_sem.at[c * Z + source])
                total = total + rz[source, :, columns].astype(jnp.float32)
            window_of(strip_of(row, z, h), c)[...] = total.astype(jnp.bfloat16)

    def product(c, p, g):
        first, size = cuts[c]
        r, q = row_of(g), group_of(p)
        base = pl.multiple_of(r * row_rows + q * step_rows, step_rows)
        left = p_ref[:, pl.ds(base, step_rows)].T
        right = s2[:, pl.ds(pl.multiple_of(base + first, LANES), size + step_rows - LANES)]
        both = jnp.dot(left, right, preferred_element_type=jnp.float32)
        for k in range(step_rows // LANES):
            piece = both[k * LANES : (k + 1) * LANES, k * LANES : k * LANES + size]
            part[pl.ds(base + k * LANES, LANES), columns_of(c)] = piece.astype(jnp.bfloat16)
        for e in range(per_step):
            j = p * per_step + e
            there = r0.at[mirrored(g) * Z + j, :, columns_of(c)]
            send(rows_of(part, strip_of(r, z_of(p, e), 1 - h), c), there, partner, ("core", c, mirrored(g), j), ("sum", c))

    def mirror_block(i, c):
        rows = pl.ds(pl.multiple_of(i * LANES, LANES), LANES)
        first, size = cuts[c]
        for d in range(max(1, first // LANES), min(half, (first + size) // LANES)):
            to = pl.multiple_of(((i + d) % blocks) * LANES, LANES)
            block = cx[rows, pl.ds(pl.multiple_of((i + d) * LANES, LANES), LANES)]
            cx[pl.ds(to, LANES), rows] = block.T

    def forward(c, g, p):
        view = window_of(strip_of(row_of(g), near(p), h), c)
        if g:
            arrived(view, ("spread", c, g, p))
        elif p:
            arrived_at(view, spread_sem.at[c * Z + near(p)])
        else:
            for k in range(1, Z):
                send_to(view, view, (row, near(k) * 2 + h), spread_sem.at[c * Z + z], ("spread", c))
        for there in reached_from(g, p, c == len(cuts) - 1 and p == Z - 1, R, low_of):
            send(view, view, (row_of(there - g), col), ("spread", c, there, p), ("spread", c))
        send(view, view, partner, ("spread_core", c, mirrored(g), p), ("spread", c))

    def block(c, g, p):
        arrived(window_of(strip_of(row_of(g), near(p), 1 - h), c), ("spread_core", c, g, p))
        if 2 * depth == LANES:
            mirror_block(row_of(g) * Z + near(p), c)

    steps_of = {"product": product, "reduce": reduce, "forward": forward, "block": block}
    for op in planned(R, Z, steps, order, mirrored, low_of, depth, cuts):
        steps_of[op[0]](*op[1:])
    if 2 * depth != LANES:
        @pl.loop(0, blocks)
        def _(i):
            for c in range(len(cuts)):
                mirror_block(i, c)

    for i in range(half, blocks):
        rows = pl.ds(i * LANES, LANES)
        over = (i + half + 1 - blocks) * LANES
        cx[rows, :over] = cx[rows, n : n + over]

    for g in range(1, R):
        arrived(x0.at[:, columns_at(row_of(g))], ("field", g))
    for index in range(TERMS - 1):
        source = x0 if index == 0 else xs.at[(index + 1) % 2]
        target = xs.at[index % 2]
        scale = 1.0 / (TERMS - index)

        product = jnp.dot(source[...], cx[:, :n], preferred_element_type=jnp.float32)
        target[...] = (x0[...].astype(jnp.float32) + scale * product).astype(jnp.bfloat16)

    source, last = xs.at[TERMS % 2], xs.at[(TERMS - 1) % 2]
    for g in reversed(range(R)):
        to = row_of(g)
        product = jnp.dot(source[...], cx[:, columns_at(to)], preferred_element_type=jnp.float32)
        value = (x0[:, columns_at(to)].astype(jnp.float32) + product).astype(jnp.bfloat16)
        if g:
            last[:, columns_at(to)] = value
            send(last.at[:, columns_at(to)], ot.at[slab_at(row), :], (to, col), ("out", g), "out")
        else:
            out_ref[slab_at(row), :] = value
    for g in reversed(range(1, R)):
        source = slab_at(row_of(g))
        arrived(ot.at[source, :], ("out", g))
        out_ref[source, :] = ot[source, :]
    for kind, (index, copies) in sends.items():
        sent = x0.at[:, : copies * row_rows] if isinstance(kind, str) else part.at[: copies * depth, columns_of(kind[1])]
        pltpu.make_async_remote_copy(
            src_ref=sent, dst_ref=sent, send_sem=send_sem.at[index],
            recv_sem=recv_sem.at[0], device_id=partner, device_id_type=MESH).wait_send()


def on_device(R, Z, mode_profiles, region_labels, gain_table, index_table, field_in):
    points, n = mode_profiles.shape
    width = n // 2 + LANES
    depth = n // (R * Z * 2)
    mine_cols = field_in.shape[1] // R
    messages = SPLITS * (2 * R * Z + 2 * (R - 1) * Z) + 2 * (R - 1)
    bf16 = jnp.bfloat16
    turned = pl.pallas_call(
        functools.partial(kernel, R, Z, n),
        out_shape=jax.ShapeDtypeStruct(field_in.shape[::-1], bf16),
        in_specs=[
            pl.BlockSpec(memory_space=pltpu.VMEM),
            pl.BlockSpec(memory_space=pltpu.SMEM),
            pl.BlockSpec(memory_space=pltpu.SMEM),
            pl.BlockSpec(memory_space=pl.ANY),
            pl.BlockSpec(memory_space=pl.ANY),
        ],
        out_specs=pl.BlockSpec(memory_space=pltpu.VMEM),
        scratch_shapes=[
            pltpu.VMEM((points, n), bf16),
            pltpu.VMEM(field_in.shape, bf16),
            pltpu.VMEM(field_in.shape[::-1], bf16),
            pltpu.VMEM((points, n + width - LANES), bf16),
            pltpu.VMEM((n, width), bf16),
            pltpu.VMEM((R * Z, depth, width), bf16),
            pltpu.VMEM(((R - 1) * Z, depth, width), bf16),
            pltpu.VMEM((Z, depth, width), bf16),
            pltpu.VMEM((n, n + width - LANES), bf16),
            pltpu.VMEM((mine_cols, n), bf16),
            pltpu.VMEM((2, mine_cols, n), bf16),
            pltpu.VMEM(field_in.shape[::-1], bf16),
            pltpu.SemaphoreType.DMA((2 * SPLITS + 2,)),
            pltpu.SemaphoreType.DMA((messages,)),
            pltpu.SemaphoreType.DMA((SPLITS * Z,)),
            pltpu.SemaphoreType.DMA((SPLITS * Z,)),
            pltpu.SemaphoreType.DMA((points // LANES,)),
            pltpu.SemaphoreType.DMA((1,)),
        ],
        compiler_params=pltpu.CompilerParams(
            collective_id=0, has_side_effects=True, vmem_limit_bytes=60 * 1024 * 1024),
    )(region_labels.reshape(-1, LANES), gain_table, index_table, mode_profiles, field_in)
    return turned.T


def solution(mesh):
    return jax.shard_map(
        functools.partial(on_device, mesh.shape["row"], mesh.shape["col"] // 2),
        mesh=mesh,
        in_specs=(P(("row", "col"), None), P(("row", "col")), P(), P(), P("row", "col")),
        out_specs=P("row", "col"),
        check_vma=False,
    )
```

```python
import functools

import jax
import jax.numpy as jnp
from jax import lax
from jax.experimental import pallas as pl
from jax.experimental.pallas import tpu as pltpu
from jax.sharding import PartitionSpec as P

TERMS = 6
LANES = 128
MESH = pl.DeviceIdType.MESH


def lowest_bit(g):
    t = 0
    while not (g >> t) & 1:
        t += 1
    return t


TILES = (2, 2, 2, 2)
SPLITS = len(TILES)
WEIGHTS = dict(
    link=102069.93, routed=2.35, extra=0.5, near=1.15, lag=0,
    reduce=2.45, reduce_cut=1.25, reduce_step=0.32, reduce_low=-0.6,
    forward=-0.89, forward_cut=-0.13, forward_far=-1.52, forward_low=-0.8,
    product=3.1, product_cut=0.92, block=4.26, block_cut=0.1,
    far_product=2.46, far_core=2.56, far_row=2.18, far_own=3.07, far_forward=1.94, far_block=2.99)


def cuts_of(width):
    edges = [width // LANES * sum(TILES[:c]) // sum(TILES) * LANES for c in range(SPLITS + 1)]
    return [(first, after - first) for first, after in zip(edges, edges[1:])]


def nearest(z, p, Z):
    edge, away = min(z, Z - 1 - z), 1 - 2 * (2 * z // Z)
    if p > 2 * edge:
        return z + away * (p - edge)
    return z + (away * (p // 2) if p % 2 == 0 else -away * ((p + 1) // 2))


def planned(R, Z, steps, order, mirrored, low_of, depth, far_rows, cuts, w):
    per_step = Z // steps
    final = (steps - 1, 0, per_step - 1)
    ops = []
    for c in range(len(cuts)):
        ops += [("product", c, p, g) for p in range(steps) for g in order]
        ops += [("reduce", c, p, g, e) for p in range(steps) for g in order for e in range(per_step)]
        ops += [("forward", c, g, p) for p in range(Z) for g in range(R)]
        ops += [("block", c, g, p) for p in range(Z) for g in range(R)]
    ops += [("far_product", 0), ("far_core", 0), ("far_row", 0), ("far_own", 0)]
    ops += [("far_forward", p) for p in range(1, Z)] + [("far_block", p) for p in range(Z)]
    at, free, start = {}, {}, 3.6

    def needs(op):
        kind, c = op[:2]
        if kind in ("product", "far_product"):
            return []
        if kind.startswith("far"):
            return {
                "far_core": [("far_core_in",)], "far_row": [("far_z_in",)], "far_own": [("far_row_in",)],
                "far_forward": [("far_spread", c), ("far_own", 0)], "far_block": [("far_partner", c), ("far_forward" if c else "far_own", c)],
            }[kind]
        if kind == "reduce":
            p, g, e = op[2:]
            j = p * per_step + e
            keys = [("product", c, p, g), ("core", c, g, j)] + [("row", c, t, g, j) for t in range(low_of(g))]
            return keys + ([("sums", c, i) for i in range(Z - 1)] if (p, g, e) == final else [])
        g, p = op[2:]
        if kind == "block":
            return [("forward", c, g, p), ("spread_core", c, g, p)]
        return [("spread", c, g, p) if (g or p) else ("reduce", c, *final)]

    def rank(op):
        kind, c = op[:2]
        if kind == "reduce":
            p, g, e = op[2:]
            return w["reduce"] + w["reduce_cut"] * c + w["reduce_step"] * p + w["reduce_low"] * low_of(g) + 0.01 * e - 0.001 * g
        if kind == "forward":
            return w["forward"] + w["forward_cut"] * c + w["forward_far"] * op[3] - w["forward_low"] * low_of(op[2])
        return w[kind] + (0.001 if kind.startswith("far") else w[kind + "_cut"]) * c

    def sent(now, link, amount, key):
        free[link] = max(free.get(link, start), now) + amount
        at[key] = free[link] + (w["near"] if link == "core" else w["routed"])

    def sent_along(now, amount, z, goal):
        way, end = (1 if goal > z else -1), now
        for k in range(z, goal, way):
            free[k, way] = max(free.get((k, way), start), now) + 2 * amount
            end = max(end, free[k, way])
        return end + w["routed"] + w["extra"] * (abs(goal - z) - 1)

    def sent_near(now, amount, key):
        ends = {(z, nearest(z, p, Z)): sent_along(now, amount, z, nearest(z, p, Z)) for p in range(1, Z) for z in range(Z)}
        for p in range(1, Z):
            at[(*key, p)] = max(ends[nearest(z, p, Z), z] for z in range(Z))

    def goal_of(z, p, e):
        return (z // per_step + 1 + p) % steps * per_step + (z % per_step + 1 + e) % per_step

    wanted, ranks = {op: needs(op) for op in ops}, {op: rank(op) for op in ops}
    now, left, done = start, list(ops), []
    far = far_rows * LANES * 2 / w["link"]
    while left:
        ripe, later = None, None
        for op in left:
            ready = 0.0
            for key in wanted[op]:
                ready = max(ready, at.get(key, 1e9))
            if op[0] in ("reduce", "forward"):
                ready += w["lag"]
            if ready <= now:
                ripe = min(ripe or (ranks[op], op), (ranks[op], op))
            elif ready < 1e9 and not ripe:
                later = min(later or (ready, ranks[op], op), (ready, ranks[op], op))
        op = ripe[1] if ripe else later[2]
        now = now if ripe else later[0]
        left.remove(op)
        done.append(op)
        kind, c = op[:2]
        tiles = cuts[c][1] / LANES if not kind.startswith("far") else 0
        strip = depth * tiles * LANES * 2 / w["link"]
        if kind == "far_product":
            now += 0.8
            sent(now, "core", far * Z / 7, ("far_core_in",))
        elif kind == "far_core":
            now += 0.1
            at["far_z_in",] = max(sent_along(now, far, z, (z + k) % Z) for k in range(1, Z) for z in range(Z))
        elif kind == "far_row":
            now += 0.1
            sent(now, "row", far * 4 / 3 * (R - 1), ("far_row_in",))
        elif kind == "far_own":
            now += 0.1
            sent_near(now, far, ("far_spread",))
            sent(now, "core", far / 7, ("far_partner", 0))
        elif kind == "far_forward":
            now += 0.05
            sent(now, "core", far / 7, ("far_partner", c))
        elif kind == "far_block":
            now += 0.2
        elif kind == "product":
            p, g = op[2:]
            now += tiles * 0.11 + 0.15
            for e in range(per_step):
                sent(now, "core", strip / 7, ("core", c, mirrored(g), p * per_step + e))
        elif kind == "reduce":
            p, g, e = op[2:]
            now += tiles * 0.025 + 0.03
            if g:
                low = low_of(g)
                sent(now, "row", strip, ("row", c, low, g ^ (1 << low), p * per_step + e))
            elif (p, g, e) != final:
                at["sums", c, p * per_step + e] = max(sent_along(now, strip, z, goal_of(z, p, e)) for z in range(Z))
        elif kind == "forward":
            g, p = op[2:]
            now += 0.08
            if g == 0 and p == 0:
                sent_near(now, strip, ("spread", c, 0))
            direct = c == len(cuts) - 1 and p == Z - 1
            for there in reached_from(g, p, direct, R, low_of):
                sent(now, "row", strip * (4 / 3 if direct else 1), ("spread", c, there, p))
            sent(now, "core", strip / 7, ("spread_core", c, mirrored(g), p))
        else:
            now += tiles * 0.075
        at[op] = now
    return done


def reached_from(g, p, direct, R, low_of):
    if direct:
        return list(reversed(range(1, R))) if g == 0 else []
    return [g | (1 << t) for t in reversed(range(low_of(g)))]


def kernel(R, Z, n, labels_ref, gain_ref, index_ref, p_hbm, f_hbm, out_ref, p_ref, f_ref, ft, s2, part, r0, rt, rz, far, f0, fz, fr, fg, cx, x0, xs, ot, send_sem, recv_sem, z_sem, spread_sem, far_sem, load_sem, small_sem):
    bits = R.bit_length() - 1
    blocks = n // LANES
    half = blocks // 2
    width = half * LANES
    depth = n // (R * Z * 2)
    far_rows = n // (4 * Z)
    mine_cols = x0.shape[0]
    row_rows = n // R
    step_rows = min(2 * LANES, row_rows)
    steps = row_rows // step_rows
    per_step = Z // steps
    row, col = lax.axis_index("row"), lax.axis_index("col")
    z, h = col // 2, col % 2
    partner = (row, z * 2 + 1 - h)

    def flip(r, t):
        mask0, mask1 = 1 << t, 1 << (bits - 1 - t)
        mask = mask0 + h * (mask1 - mask0)
        return r + mask * (1 - 2 * ((r // mask) % 2))

    def row_of(g):
        r = row
        for t in range(bits):
            if (g >> t) & 1:
                r = flip(r, t)
        return r

    def mirrored(g):
        return sum(((g >> t) & 1) << (bits - 1 - t) for t in range(bits))

    def low_of(g):
        return lowest_bit(g) if g else bits

    def group_of(p):
        return (z // per_step + 1 + p) % steps

    def z_of(p, e):
        return group_of(p) * per_step + (z % per_step + 1 + e) % per_step

    def near(p):
        if p == 0:
            return z
        edge = jnp.minimum(z, Z - 1 - z)
        away = 1 - 2 * (2 * z // Z)
        both_sides = away * (p // 2) if p % 2 == 0 else -away * ((p + 1) // 2)
        return z + jnp.where(p <= 2 * edge, both_sides, away * (p - edge))

    def strip_of(r, zz, hh):
        return (r * Z + zz) * 2 + hh

    cuts = cuts_of(width)

    def columns_of(c):
        return pl.ds(*cuts[c])

    def rows_of(ref, s, c):
        return ref.at[pl.ds(pl.multiple_of(s * depth, depth), depth), columns_of(c)]

    def window_of(s, c):
        first, size = cuts[c]
        start = pl.multiple_of((s * depth // LANES) * LANES + first, LANES)
        return cx.at[pl.ds(pl.multiple_of(s * depth, depth), depth), pl.ds(start, size)]

    ids, sends = {}, {}

    def slot(key):
        return recv_sem.at[ids.setdefault(key, len(ids))]

    def send_to(src, dst, device, sem, kind):
        index, copies = sends.get(kind, (len(sends), 0))
        sends[kind] = index, copies + 1
        pltpu.make_async_remote_copy(
            src_ref=src, dst_ref=dst, send_sem=send_sem.at[index],
            recv_sem=sem, device_id=device, device_id_type=MESH).start()

    def send(src, dst, device, key, kind):
        send_to(src, dst, device, slot(key), kind)

    def arrived_at(ref, sem):
        pltpu.make_async_remote_copy(
            src_ref=ref, dst_ref=ref, send_sem=send_sem.at[0],
            recv_sem=sem, device_id=partner, device_id_type=MESH).wait_recv()

    def arrived(ref, key):
        arrived_at(ref, slot(key))

    rows_at_once = LANES
    loads = p_ref.shape[0] // rows_at_once

    def load(i):
        rows = pl.ds(i * rows_at_once, rows_at_once)
        return pltpu.make_async_copy(p_hbm.at[rows, :], p_ref.at[rows, :], load_sem.at[i])

    load_field = pltpu.make_async_copy(f_hbm, f_ref, small_sem.at[0])
    load(0).start()
    load_field.start()
    for i in range(1, loads):
        load(i).start()

    barrier = pltpu.get_barrier_semaphore()
    peers = [(row_of(g), col) for g in range(1, R)]
    peers += [(row, ((z + k) % Z) * 2 + h) for k in range(1, Z)] + [partner]
    for peer in peers:
        pl.semaphore_signal(barrier, inc=1, device_id=peer, device_id_type=MESH)

    def columns_at(r):
        return pl.ds(pl.multiple_of(r * row_rows, row_rows), row_rows)

    def slab_at(r):
        return pl.ds(pl.multiple_of(r * mine_cols, mine_cols), mine_cols)

    labels = labels_ref[...]
    weight = jnp.zeros(labels.shape, jnp.float32)
    for region in range(gain_ref.shape[0]):
        weight = jnp.where(labels == region, gain_ref[region] + index_ref[region], weight)
    for i in range(loads):
        rows = pl.ds(i * rows_at_once, rows_at_once)
        along = jnp.broadcast_to(weight[i : i + 1, :], (LANES, LANES)).T
        load(i).wait()
        for c in range(n // LANES):
            columns = pl.ds(c * LANES, LANES)
            scaled = (p_ref[rows, columns].astype(jnp.float32) * along).astype(jnp.bfloat16)
            s2[rows, columns] = scaled
            if c * LANES < width - LANES:
                s2[rows, pl.ds(n + c * LANES, LANES)] = scaled
        if i == loads // 2:
            load_field.wait()
            ft[...] = f_ref[...].T

    pl.semaphore_wait(barrier, len(peers))
    for g in range(1, R):
        to = row_of(g)
        send(ft.at[slab_at(to), :], x0.at[:, columns_at(row)], (to, col), ("field", g), "field")
    x0[:, columns_at(row)] = ft[slab_at(row), :]

    order = sorted(range(R), key=lambda g: (low_of(g), -g))
    stage_slot = {}
    for t in range(bits):
        for g in range(R):
            if g % (2 << t) == 0:
                stage_slot[t, g] = len(stage_slot)

    met = set()

    def reduce(c, p, g, e):
        low, j = low_of(g), p * per_step + e
        zz, columns = z_of(p, e), columns_of(c)
        if (c, p, g) not in met:
            met.add((c, p, g))
            arrived(r0.at[g * Z + p * per_step : g * Z + (p + 1) * per_step, :, columns], ("core", c, g, p))
        own = rows_of(part, strip_of(row_of(g), zz, h), c)
        total = own[...].astype(jnp.float32) + r0[g * Z + j, :, columns].astype(jnp.float32)
        for t in range(low):
            piece = rt.at[stage_slot[t, g] * Z + j, :, columns]
            arrived(piece, ("row", c, t, g, j))
            total = total + piece[...].astype(jnp.float32)
        if g:
            own[...] = total.astype(jnp.bfloat16)
            seen = g ^ (1 << low)
            send(own, rt.at[stage_slot[low, seen] * Z + j, :, columns], (flip(row, low), col), ("row", c, low, seen, j), ("sum", c))
        elif j < Z - 1:
            own[...] = total.astype(jnp.bfloat16)
            send_to(own, rz.at[z, :, columns], (row, zz * 2 + h), z_sem.at[c * Z + z], ("sum", c))
        else:
            for i in range(1, Z):
                source = (z + i) % Z
                arrived_at(rz.at[source, :, columns], z_sem.at[c * Z + source])
                total = total + rz[source, :, columns].astype(jnp.float32)
            window_of(strip_of(row, z, h), c)[...] = total.astype(jnp.bfloat16)

    def product(c, p, g):
        first, size = cuts[c]
        r, q = row_of(g), group_of(p)
        base = pl.multiple_of(r * row_rows + q * step_rows, step_rows)
        left = p_ref[:, pl.ds(base, step_rows)].T
        right = s2[:, pl.ds(pl.multiple_of(base + first, LANES), size + step_rows - LANES)]
        both = jnp.dot(left, right, preferred_element_type=jnp.float32)
        for k in range(step_rows // LANES):
            piece = both[k * LANES : (k + 1) * LANES, k * LANES : k * LANES + size]
            part[pl.ds(base + k * LANES, LANES), columns_of(c)] = piece.astype(jnp.bfloat16)
        for e in range(per_step):
            j = p * per_step + e
            there = r0.at[mirrored(g) * Z + j, :, columns_of(c)]
            send(rows_of(part, strip_of(r, z_of(p, e), 1 - h), c), there, partner, ("core", c, mirrored(g), p), ("sum", c))

    def mirror_block(i, c):
        rows = pl.ds(pl.multiple_of(i * LANES, LANES), LANES)
        first, size = cuts[c]
        for d in range(max(1, first // LANES), min(half, (first + size) // LANES)):
            to = pl.multiple_of(((i + d) % blocks) * LANES, LANES)
            block = cx[rows, pl.ds(pl.multiple_of((i + d) * LANES, LANES), LANES)]
            cx[pl.ds(to, LANES), rows] = block.T

    def forward(c, g, p):
        view = window_of(strip_of(row_of(g), near(p), h), c)
        if g:
            arrived(view, ("spread", c, g, p))
        elif p:
            arrived_at(view, spread_sem.at[c * Z + near(p)])
        else:
            for k in range(1, Z):
                send_to(view, view, (row, near(k) * 2 + h), spread_sem.at[c * Z + z], ("spread", c))
        for there in reached_from(g, p, c == len(cuts) - 1 and p == Z - 1, R, low_of):
            send(view, view, (row_of(there - g), col), ("spread", c, there, p), ("spread", c))
        send(view, view, partner, ("spread_core", c, mirrored(g), p), ("spread", c))

    def block(c, g, p):
        arrived(window_of(strip_of(row_of(g), near(p), 1 - h), c), ("spread_core", c, g, p))
        if 2 * depth == LANES:
            mirror_block(row_of(g) * Z + near(p), c)

    def far_at(hh, zz, count=1):
        return pl.ds(pl.multiple_of((hh * Z + zz) * far_rows, far_rows), count * far_rows)

    def far_product(_):
        for hh in (1 - h, h):
            for k in range(half // 2):
                base = pl.multiple_of((hh * (half // 2) + k) * LANES, LANES)
                left = p_ref[:, pl.ds(base, LANES)].T
                right = s2[:, pl.ds(pl.multiple_of(base + half * LANES, LANES), LANES)]
                far[pl.ds(base, LANES), :] = jnp.dot(left, right, preferred_element_type=jnp.float32).astype(jnp.bfloat16)
        send(far.at[far_at(1 - h, 0, Z), :], f0, partner, ("far_core",), "far_core")

    def far_core(_):
        arrived(f0, ("far_core",))
        rows = far_at(h, 0, Z)
        far[rows, :] = (far[rows, :].astype(jnp.float32) + f0[...].astype(jnp.float32)).astype(jnp.bfloat16)
        for k in range(1, Z):
            zz = (z + k) % Z
            send_to(far.at[far_at(h, zz), :], fz.at[z], (row, zz * 2 + h), far_sem.at[z], "far")

    def far_row(_):
        rows = far_at(h, z)
        total = far[rows, :].astype(jnp.float32)
        for k in range(1, Z):
            source = (z + k) % Z
            arrived_at(fz.at[source], far_sem.at[source])
            total = total + fz[source].astype(jnp.float32)
        far[rows, :] = total.astype(jnp.bfloat16)
        for g in reversed(range(1, R)):
            send(far.at[rows, :], fr.at[g], (row_of(g), col), ("far_row", g), "far")

    def far_own(_):
        rows = far_at(h, z)
        total = far[rows, :].astype(jnp.float32)
        for g in range(1, R):
            arrived(fr.at[g], ("far_row", g))
            total = total + fr[g].astype(jnp.float32)
        fg[rows, :] = total.astype(jnp.bfloat16)
        view = fg.at[rows, :]
        for k in range(1, Z):
            send_to(view, view, (row, near(k) * 2 + h), far_sem.at[Z + z], "far")
        send(view, view, partner, ("far_partner", 0), "far")

    def far_forward(p):
        view = fg.at[far_at(h, near(p)), :]
        arrived_at(view, far_sem.at[Z + near(p)])
        send(view, view, partner, ("far_partner", p), "far")

    def place_far(i):
        here, there = pl.multiple_of(i * LANES, LANES), pl.multiple_of((i + half) * LANES, LANES)
        piece = fg[pl.ds(here, LANES), :]
        cx[pl.ds(here, LANES), pl.ds(there, LANES)] = piece
        cx[pl.ds(there, LANES), pl.ds(here, LANES)] = piece.T

    def far_block(p):
        arrived(fg.at[far_at(1 - h, near(p)), :], ("far_partner", p))
        if far_rows == LANES:
            for hh in range(2):
                place_far(hh * Z + near(p))

    steps_of = {"far_product": far_product, "far_core": far_core, "far_row": far_row, "far_own": far_own}
    steps_of |= {"far_forward": far_forward, "far_block": far_block}
    steps_of |= {"product": product, "reduce": reduce, "forward": forward, "block": block}
    for op in planned(R, Z, steps, order, mirrored, low_of, depth, far_rows, cuts, WEIGHTS):
        steps_of[op[0]](*op[1:])
    if 2 * depth != LANES:
        @pl.loop(0, blocks)
        def _(i):
            for c in range(len(cuts)):
                mirror_block(i, c)

    if far_rows != LANES:
        pl.loop(0, half)(place_far)

    for i in range(half + 1, blocks):
        rows = pl.ds(i * LANES, LANES)
        over = (i + half - blocks) * LANES
        cx[rows, :over] = cx[rows, n : n + over]

    for g in range(1, R):
        arrived(x0.at[:, columns_at(row_of(g))], ("field", g))
    for index in range(TERMS - 1):
        source = x0 if index == 0 else xs.at[(index + 1) % 2]
        target = xs.at[index % 2]
        scale = 1.0 / (TERMS - index)

        product = jnp.dot(source[...], cx[:, :n], preferred_element_type=jnp.float32)
        target[...] = (x0[...].astype(jnp.float32) + scale * product).astype(jnp.bfloat16)

    source, last = xs.at[TERMS % 2], xs.at[(TERMS - 1) % 2]
    for g in reversed(range(R)):
        to = row_of(g)
        product = jnp.dot(source[...], cx[:, columns_at(to)], preferred_element_type=jnp.float32)
        value = (x0[:, columns_at(to)].astype(jnp.float32) + product).astype(jnp.bfloat16)
        if g:
            last[:, columns_at(to)] = value
            send(last.at[:, columns_at(to)], ot.at[slab_at(row), :], (to, col), ("out", g), "out")
        else:
            out_ref[slab_at(row), :] = value
    for g in reversed(range(1, R)):
        source = slab_at(row_of(g))
        arrived(ot.at[source, :], ("out", g))
        out_ref[source, :] = ot[source, :]
    for kind, (index, copies) in sends.items():
        if kind in ("field", "out"):
            sent = x0.at[:, : copies * row_rows]
        elif kind == "far_core":
            sent = f0
        elif kind == "far":
            sent = part.at[: copies * far_rows, :LANES]
        else:
            sent = part.at[: copies * depth, columns_of(kind[1])]
        pltpu.make_async_remote_copy(
            src_ref=sent, dst_ref=sent, send_sem=send_sem.at[index],
            recv_sem=recv_sem.at[0], device_id=partner, device_id_type=MESH).wait_send()


def on_device(R, Z, mode_profiles, region_labels, gain_table, index_table, field_in):
    points, n = mode_profiles.shape
    width = n // 2
    far_rows = n // (4 * Z)
    depth = n // (R * Z * 2)
    mine_cols = field_in.shape[1] // R
    steps = max(1, n // R // (2 * LANES))
    messages = SPLITS * (R * steps + R * Z + 2 * (R - 1) * Z) + 3 * (R - 1) + 1 + Z
    bf16 = jnp.bfloat16
    turned = pl.pallas_call(
        functools.partial(kernel, R, Z, n),
        out_shape=jax.ShapeDtypeStruct(field_in.shape[::-1], bf16),
        in_specs=[
            pl.BlockSpec(memory_space=pltpu.VMEM),
            pl.BlockSpec(memory_space=pltpu.SMEM),
            pl.BlockSpec(memory_space=pltpu.SMEM),
            pl.BlockSpec(memory_space=pl.ANY),
            pl.BlockSpec(memory_space=pl.ANY),
        ],
        out_specs=pl.BlockSpec(memory_space=pltpu.VMEM),
        scratch_shapes=[
            pltpu.VMEM((points, n), bf16),
            pltpu.VMEM(field_in.shape, bf16),
            pltpu.VMEM(field_in.shape[::-1], bf16),
            pltpu.VMEM((points, n + width - LANES), bf16),
            pltpu.VMEM((n, width), bf16),
            pltpu.VMEM((R * Z, depth, width), bf16),
            pltpu.VMEM(((R - 1) * Z, depth, width), bf16),
            pltpu.VMEM((Z, depth, width), bf16),
            pltpu.VMEM((n // 2, LANES), bf16),
            pltpu.VMEM((Z * far_rows, LANES), bf16),
            pltpu.VMEM((Z, far_rows, LANES), bf16),
            pltpu.VMEM((R, far_rows, LANES), bf16),
            pltpu.VMEM((n // 2, LANES), bf16),
            pltpu.VMEM((n, n + width - LANES), bf16),
            pltpu.VMEM((mine_cols, n), bf16),
            pltpu.VMEM((2, mine_cols, n), bf16),
            pltpu.VMEM(field_in.shape[::-1], bf16),
            pltpu.SemaphoreType.DMA((2 * SPLITS + 4,)),
            pltpu.SemaphoreType.DMA((messages,)),
            pltpu.SemaphoreType.DMA((SPLITS * Z,)),
            pltpu.SemaphoreType.DMA((SPLITS * Z,)),
            pltpu.SemaphoreType.DMA((2 * Z,)),
            pltpu.SemaphoreType.DMA((points // LANES,)),
            pltpu.SemaphoreType.DMA((1,)),
        ],
        compiler_params=pltpu.CompilerParams(
            collective_id=0, has_side_effects=True, vmem_limit_bytes=60 * 1024 * 1024),
    )(region_labels.reshape(-1, LANES), gain_table, index_table, mode_profiles, field_in)
    return turned.T


def solution(mesh):
    return jax.shard_map(
        functools.partial(on_device, mesh.shape["row"], mesh.shape["col"] // 2),
        mesh=mesh,
        in_specs=(P(("row", "col"), None), P(("row", "col")), P(), P(), P("row", "col")),
        out_specs=P("row", "col"),
        check_vma=False,
    )
```

```python
import functools

import jax
import jax.numpy as jnp
from jax import lax
from jax.experimental import pallas as pl
from jax.experimental.pallas import tpu as pltpu
from jax.sharding import PartitionSpec as P

TERMS = 6
LANES = 128
MESH = pl.DeviceIdType.MESH


def lowest_bit(g):
    t = 0
    while not (g >> t) & 1:
        t += 1
    return t


TILES = (2, 2, 2, 2)
SPLITS = len(TILES)
WEIGHTS = dict(
    link=102069.93, routed=2.35, extra=0.5, near=1.15, lag=0,
    reduce=2.45, reduce_cut=1.25, reduce_step=0.32, reduce_low=-0.6,
    forward=-0.89, forward_cut=-0.13, forward_far=-1.52, forward_low=-0.8,
    product=3.1, product_cut=0.92, block=4.26, block_cut=0.1,
    far_product=2.46, far_core=2.56, far_row=2.18, far_own=3.07, far_forward=1.94, far_block=2.99)


def cuts_of(width):
    edges = [width // LANES * sum(TILES[:c]) // sum(TILES) * LANES for c in range(SPLITS + 1)]
    return [(first, after - first) for first, after in zip(edges, edges[1:])]


def nearest(z, p, Z):
    edge, away = min(z, Z - 1 - z), 1 - 2 * (2 * z // Z)
    if p > 2 * edge:
        return z + away * (p - edge)
    return z + (away * (p // 2) if p % 2 == 0 else -away * ((p + 1) // 2))


def planned(R, Z, steps, order, mirrored, low_of, depth, far_rows, cuts, w):
    per_step = Z // steps
    final = (steps - 1, 0, per_step - 1)
    ops = []
    for c in range(len(cuts)):
        ops += [("product", c, p, g) for p in range(steps) for g in order]
        ops += [("reduce", c, p, g, e) for p in range(steps) for g in order for e in range(per_step)]
        ops += [("forward", c, g, p) for p in range(Z) for g in range(R)]
        ops += [("block", c, g, p) for p in range(Z) for g in range(R)]
    ops += [("far_product", 0), ("far_core", 0), ("far_row", 0), ("far_own", 0)]
    ops += [("far_forward", p) for p in range(1, Z)] + [("far_block", p) for p in range(Z)]
    at, free, start = {}, {}, 3.6

    def needs(op):
        kind, c = op[:2]
        if kind in ("product", "far_product"):
            return []
        if kind.startswith("far"):
            return {
                "far_core": [("far_core_in",)], "far_row": [("far_z_in",)], "far_own": [("far_row_in",)],
                "far_forward": [("far_spread", c), ("far_own", 0)], "far_block": [("far_partner", c), ("far_forward" if c else "far_own", c)],
            }[kind]
        if kind == "reduce":
            p, g, e = op[2:]
            j = p * per_step + e
            keys = [("product", c, p, g), ("core", c, g, j)] + [("row", c, t, g, j) for t in range(low_of(g))]
            return keys + ([("sums", c, i) for i in range(Z - 1)] if (p, g, e) == final else [])
        g, p = op[2:]
        if kind == "block":
            return [("forward", c, g, p), ("spread_core", c, g, p)]
        return [("spread", c, g, p) if (g or p) else ("reduce", c, *final)]

    def rank(op):
        kind, c = op[:2]
        if kind == "reduce":
            p, g, e = op[2:]
            return w["reduce"] + w["reduce_cut"] * c + w["reduce_step"] * p + w["reduce_low"] * low_of(g) + 0.01 * e - 0.001 * g
        if kind == "forward":
            return w["forward"] + w["forward_cut"] * c + w["forward_far"] * op[3] - w["forward_low"] * low_of(op[2])
        return w[kind] + (0.001 if kind.startswith("far") else w[kind + "_cut"]) * c

    def sent(now, link, amount, key):
        free[link] = max(free.get(link, start), now) + amount
        at[key] = free[link] + (w["near"] if link == "core" else w["routed"])

    def sent_along(now, amount, z, goal):
        way, end = (1 if goal > z else -1), now
        for k in range(z, goal, way):
            free[k, way] = max(free.get((k, way), start), now) + 2 * amount
            end = max(end, free[k, way])
        return end + w["routed"] + w["extra"] * (abs(goal - z) - 1)

    def sent_near(now, amount, key):
        ends = {(z, nearest(z, p, Z)): sent_along(now, amount, z, nearest(z, p, Z)) for p in range(1, Z) for z in range(Z)}
        for p in range(1, Z):
            at[(*key, p)] = max(ends[nearest(z, p, Z), z] for z in range(Z))

    def goal_of(z, p, e):
        return (z // per_step + 1 + p) % steps * per_step + (z % per_step + 1 + e) % per_step

    wanted, ranks = {op: needs(op) for op in ops}, {op: rank(op) for op in ops}
    now, left, done = start, list(ops), []
    far = far_rows * LANES * 2 / w["link"]
    while left:
        ripe, later = None, None
        for op in left:
            ready = 0.0
            for key in wanted[op]:
                ready = max(ready, at.get(key, 1e9))
            if op[0] in ("reduce", "forward"):
                ready += w["lag"]
            if ready <= now:
                ripe = min(ripe or (ranks[op], op), (ranks[op], op))
            elif ready < 1e9 and not ripe:
                later = min(later or (ready, ranks[op], op), (ready, ranks[op], op))
        op = ripe[1] if ripe else later[2]
        now = now if ripe else later[0]
        left.remove(op)
        done.append(op)
        kind, c = op[:2]
        tiles = cuts[c][1] / LANES if not kind.startswith("far") else 0
        strip = depth * tiles * LANES * 2 / w["link"]
        if kind == "far_product":
            now += 0.8
            sent(now, "core", far * Z / 7, ("far_core_in",))
        elif kind == "far_core":
            now += 0.1
            at["far_z_in",] = max(sent_along(now, far, z, (z + k) % Z) for k in range(1, Z) for z in range(Z))
        elif kind == "far_row":
            now += 0.1
            sent(now, "row", far * 4 / 3 * (R - 1), ("far_row_in",))
        elif kind == "far_own":
            now += 0.1
            sent_near(now, far, ("far_spread",))
            sent(now, "core", far / 7, ("far_partner", 0))
        elif kind == "far_forward":
            now += 0.05
            sent(now, "core", far / 7, ("far_partner", c))
        elif kind == "far_block":
            now += 0.2
        elif kind == "product":
            p, g = op[2:]
            now += tiles * 0.11 + 0.15
            for e in range(per_step):
                sent(now, "core", strip / 7, ("core", c, mirrored(g), p * per_step + e))
        elif kind == "reduce":
            p, g, e = op[2:]
            now += tiles * 0.025 + 0.03
            if g:
                low = low_of(g)
                sent(now, "row", strip, ("row", c, low, g ^ (1 << low), p * per_step + e))
            elif (p, g, e) != final:
                at["sums", c, p * per_step + e] = max(sent_along(now, strip, z, goal_of(z, p, e)) for z in range(Z))
        elif kind == "forward":
            g, p = op[2:]
            now += 0.08
            if g == 0 and p == 0:
                sent_near(now, strip, ("spread", c, 0))
            direct = c == len(cuts) - 1 and p == Z - 1
            for there in reached_from(g, p, direct, R, low_of):
                sent(now, "row", strip * (4 / 3 if direct else 1), ("spread", c, there, p))
            sent(now, "core", strip / 7, ("spread_core", c, mirrored(g), p))
        else:
            now += tiles * 0.075
        at[op] = now
    return done


def reached_from(g, p, direct, R, low_of):
    if direct:
        return list(reversed(range(1, R))) if g == 0 else []
    return [g | (1 << t) for t in reversed(range(low_of(g)))]


def kernel(R, Z, n, labels_hbm, gain_hbm, index_hbm, p_hbm, f_hbm, out_ref, p_ref, labels_ref, gain_ref, index_ref, f_ref, ft, s2, part, r0, rt, rz, far, f0, fz, fr, fg, cx, x0, xs, ot, send_sem, recv_sem, z_sem, spread_sem, far_sem, load_sem, small_sem):
    bits = R.bit_length() - 1
    blocks = n // LANES
    half = blocks // 2
    width = half * LANES
    depth = n // (R * Z * 2)
    far_rows = n // (4 * Z)
    mine_cols = x0.shape[0]
    row_rows = n // R
    step_rows = min(2 * LANES, row_rows)
    steps = row_rows // step_rows
    per_step = Z // steps
    row, col = lax.axis_index("row"), lax.axis_index("col")
    z, h = col // 2, col % 2
    partner = (row, z * 2 + 1 - h)

    def flip(r, t):
        mask0, mask1 = 1 << t, 1 << (bits - 1 - t)
        mask = mask0 + h * (mask1 - mask0)
        return r + mask * (1 - 2 * ((r // mask) % 2))

    def row_of(g):
        r = row
        for t in range(bits):
            if (g >> t) & 1:
                r = flip(r, t)
        return r

    def mirrored(g):
        return sum(((g >> t) & 1) << (bits - 1 - t) for t in range(bits))

    def low_of(g):
        return lowest_bit(g) if g else bits

    def group_of(p):
        return (z // per_step + 1 + p) % steps

    def z_of(p, e):
        return group_of(p) * per_step + (z % per_step + 1 + e) % per_step

    def near(p):
        if p == 0:
            return z
        edge = jnp.minimum(z, Z - 1 - z)
        away = 1 - 2 * (2 * z // Z)
        both_sides = away * (p // 2) if p % 2 == 0 else -away * ((p + 1) // 2)
        return z + jnp.where(p <= 2 * edge, both_sides, away * (p - edge))

    def strip_of(r, zz, hh):
        return (r * Z + zz) * 2 + hh

    cuts = cuts_of(width)

    def columns_of(c):
        return pl.ds(*cuts[c])

    def rows_of(ref, s, c):
        return ref.at[pl.ds(pl.multiple_of(s * depth, depth), depth), columns_of(c)]

    def window_of(s, c):
        first, size = cuts[c]
        start = pl.multiple_of((s * depth // LANES) * LANES + first, LANES)
        return cx.at[pl.ds(pl.multiple_of(s * depth, depth), depth), pl.ds(start, size)]

    ids, sends = {}, {}

    def slot(key):
        return recv_sem.at[ids.setdefault(key, len(ids))]

    def send_to(src, dst, device, sem, kind):
        index, copies = sends.get(kind, (len(sends), 0))
        sends[kind] = index, copies + 1
        pltpu.make_async_remote_copy(
            src_ref=src, dst_ref=dst, send_sem=send_sem.at[index],
            recv_sem=sem, device_id=device, device_id_type=MESH).start()

    def send(src, dst, device, key, kind):
        send_to(src, dst, device, slot(key), kind)

    def arrived_at(ref, sem):
        pltpu.make_async_remote_copy(
            src_ref=ref, dst_ref=ref, send_sem=send_sem.at[0],
            recv_sem=sem, device_id=partner, device_id_type=MESH).wait_recv()

    def arrived(ref, key):
        arrived_at(ref, slot(key))

    rows_at_once = LANES
    loads = p_ref.shape[0] // rows_at_once

    def load(i):
        rows = pl.ds(i * rows_at_once, rows_at_once)
        return pltpu.make_async_copy(p_hbm.at[rows, :], p_ref.at[rows, :], load_sem.at[i])

    load_field = pltpu.make_async_copy(f_hbm, f_ref, small_sem.at[0])
    small = [(labels_hbm, labels_ref), (gain_hbm, gain_ref), (index_hbm, index_ref)]
    small = [pltpu.make_async_copy(here, there, small_sem.at[1 + k]) for k, (here, there) in enumerate(small)]
    for copy in small:
        copy.start()
    load(0).start()
    load_field.start()
    for i in range(1, loads):
        load(i).start()

    barrier = pltpu.get_barrier_semaphore()
    peers = [(row_of(g), col) for g in range(1, R)]
    peers += [(row, ((z + k) % Z) * 2 + h) for k in range(1, Z)] + [partner]
    for peer in peers:
        pl.semaphore_signal(barrier, inc=1, device_id=peer, device_id_type=MESH)

    def columns_at(r):
        return pl.ds(pl.multiple_of(r * row_rows, row_rows), row_rows)

    def slab_at(r):
        return pl.ds(pl.multiple_of(r * mine_cols, mine_cols), mine_cols)

    for copy in small:
        copy.wait()
    labels = labels_ref[...]
    weight = jnp.zeros(labels.shape, jnp.float32)
    for region in range(gain_ref.shape[0]):
        weight = jnp.where(labels == region, gain_ref[region] + index_ref[region], weight)
    for i in range(loads):
        rows = pl.ds(i * rows_at_once, rows_at_once)
        along = jnp.broadcast_to(weight[i : i + 1, :], (LANES, LANES)).T
        load(i).wait()
        for c in range(n // LANES):
            columns = pl.ds(c * LANES, LANES)
            scaled = (p_ref[rows, columns].astype(jnp.float32) * along).astype(jnp.bfloat16)
            s2[rows, columns] = scaled
            if c * LANES < width - LANES:
                s2[rows, pl.ds(n + c * LANES, LANES)] = scaled
        if i == loads // 2:
            load_field.wait()
            ft[...] = f_ref[...].T

    pl.semaphore_wait(barrier, len(peers))
    for g in range(1, R):
        to = row_of(g)
        send(ft.at[slab_at(to), :], x0.at[:, columns_at(row)], (to, col), ("field", g), "field")
    x0[:, columns_at(row)] = ft[slab_at(row), :]

    order = sorted(range(R), key=lambda g: (low_of(g), -g))
    stage_slot = {}
    for t in range(bits):
        for g in range(R):
            if g % (2 << t) == 0:
                stage_slot[t, g] = len(stage_slot)

    met = set()

    def reduce(c, p, g, e):
        low, j = low_of(g), p * per_step + e
        zz, columns = z_of(p, e), columns_of(c)
        if (c, p, g) not in met:
            met.add((c, p, g))
            arrived(r0.at[g * Z + p * per_step : g * Z + (p + 1) * per_step, :, columns], ("core", c, g, p))
        own = rows_of(part, strip_of(row_of(g), zz, h), c)
        total = own[...].astype(jnp.float32) + r0[g * Z + j, :, columns].astype(jnp.float32)
        for t in range(low):
            piece = rt.at[stage_slot[t, g] * Z + j, :, columns]
            arrived(piece, ("row", c, t, g, j))
            total = total + piece[...].astype(jnp.float32)
        if g:
            own[...] = total.astype(jnp.bfloat16)
            seen = g ^ (1 << low)
            send(own, rt.at[stage_slot[low, seen] * Z + j, :, columns], (flip(row, low), col), ("row", c, low, seen, j), ("sum", c))
        elif j < Z - 1:
            own[...] = total.astype(jnp.bfloat16)
            send_to(own, rz.at[z, :, columns], (row, zz * 2 + h), z_sem.at[c * Z + z], ("sum", c))
        else:
            for i in range(1, Z):
                source = (z + i) % Z
                arrived_at(rz.at[source, :, columns], z_sem.at[c * Z + source])
                total = total + rz[source, :, columns].astype(jnp.float32)
            window_of(strip_of(row, z, h), c)[...] = total.astype(jnp.bfloat16)

    def product(c, p, g):
        first, size = cuts[c]
        r, q = row_of(g), group_of(p)
        base = pl.multiple_of(r * row_rows + q * step_rows, step_rows)
        left = p_ref[:, pl.ds(base, step_rows)].T
        right = s2[:, pl.ds(pl.multiple_of(base + first, LANES), size + step_rows - LANES)]
        both = jnp.dot(left, right, preferred_element_type=jnp.float32)
        for k in range(step_rows // LANES):
            piece = both[k * LANES : (k + 1) * LANES, k * LANES : k * LANES + size]
            part[pl.ds(base + k * LANES, LANES), columns_of(c)] = piece.astype(jnp.bfloat16)
        for e in range(per_step):
            j = p * per_step + e
            there = r0.at[mirrored(g) * Z + j, :, columns_of(c)]
            send(rows_of(part, strip_of(r, z_of(p, e), 1 - h), c), there, partner, ("core", c, mirrored(g), p), ("sum", c))

    def mirror_block(i, c):
        rows = pl.ds(pl.multiple_of(i * LANES, LANES), LANES)
        first, size = cuts[c]
        for d in range(max(1, first // LANES), min(half, (first + size) // LANES)):
            to = pl.multiple_of(((i + d) % blocks) * LANES, LANES)
            block = cx[rows, pl.ds(pl.multiple_of((i + d) * LANES, LANES), LANES)]
            cx[pl.ds(to, LANES), rows] = block.T

    def forward(c, g, p):
        view = window_of(strip_of(row_of(g), near(p), h), c)
        if g:
            arrived(view, ("spread", c, g, p))
        elif p:
            arrived_at(view, spread_sem.at[c * Z + near(p)])
        else:
            for k in range(1, Z):
                send_to(view, view, (row, near(k) * 2 + h), spread_sem.at[c * Z + z], ("spread", c))
        for there in reached_from(g, p, c == len(cuts) - 1 and p == Z - 1, R, low_of):
            send(view, view, (row_of(there - g), col), ("spread", c, there, p), ("spread", c))
        send(view, view, partner, ("spread_core", c, mirrored(g), p), ("spread", c))

    def block(c, g, p):
        arrived(window_of(strip_of(row_of(g), near(p), 1 - h), c), ("spread_core", c, g, p))
        if 2 * depth == LANES:
            mirror_block(row_of(g) * Z + near(p), c)

    def far_at(hh, zz, count=1):
        return pl.ds(pl.multiple_of((hh * Z + zz) * far_rows, far_rows), count * far_rows)

    def far_product(_):
        for hh in (1 - h, h):
            for k in range(half // 2):
                base = pl.multiple_of((hh * (half // 2) + k) * LANES, LANES)
                left = p_ref[:, pl.ds(base, LANES)].T
                right = s2[:, pl.ds(pl.multiple_of(base + half * LANES, LANES), LANES)]
                far[pl.ds(base, LANES), :] = jnp.dot(left, right, preferred_element_type=jnp.float32).astype(jnp.bfloat16)
        send(far.at[far_at(1 - h, 0, Z), :], f0, partner, ("far_core",), "far_core")

    def far_core(_):
        arrived(f0, ("far_core",))
        rows = far_at(h, 0, Z)
        far[rows, :] = (far[rows, :].astype(jnp.float32) + f0[...].astype(jnp.float32)).astype(jnp.bfloat16)
        for k in range(1, Z):
            zz = (z + k) % Z
            send_to(far.at[far_at(h, zz), :], fz.at[z], (row, zz * 2 + h), far_sem.at[z], "far")

    def far_row(_):
        rows = far_at(h, z)
        total = far[rows, :].astype(jnp.float32)
        for k in range(1, Z):
            source = (z + k) % Z
            arrived_at(fz.at[source], far_sem.at[source])
            total = total + fz[source].astype(jnp.float32)
        far[rows, :] = total.astype(jnp.bfloat16)
        for g in reversed(range(1, R)):
            send(far.at[rows, :], fr.at[g], (row_of(g), col), ("far_row", g), "far")

    def far_own(_):
        rows = far_at(h, z)
        total = far[rows, :].astype(jnp.float32)
        for g in range(1, R):
            arrived(fr.at[g], ("far_row", g))
            total = total + fr[g].astype(jnp.float32)
        fg[rows, :] = total.astype(jnp.bfloat16)
        view = fg.at[rows, :]
        for k in range(1, Z):
            send_to(view, view, (row, near(k) * 2 + h), far_sem.at[Z + z], "far")
        send(view, view, partner, ("far_partner", 0), "far")

    def far_forward(p):
        view = fg.at[far_at(h, near(p)), :]
        arrived_at(view, far_sem.at[Z + near(p)])
        send(view, view, partner, ("far_partner", p), "far")

    def place_far(i):
        here, there = pl.multiple_of(i * LANES, LANES), pl.multiple_of((i + half) * LANES, LANES)
        piece = fg[pl.ds(here, LANES), :]
        cx[pl.ds(here, LANES), pl.ds(there, LANES)] = piece
        cx[pl.ds(there, LANES), pl.ds(here, LANES)] = piece.T

    def far_block(p):
        arrived(fg.at[far_at(1 - h, near(p)), :], ("far_partner", p))
        if far_rows == LANES:
            for hh in range(2):
                place_far(hh * Z + near(p))

    steps_of = {"far_product": far_product, "far_core": far_core, "far_row": far_row, "far_own": far_own}
    steps_of |= {"far_forward": far_forward, "far_block": far_block}
    steps_of |= {"product": product, "reduce": reduce, "forward": forward, "block": block}
    for op in planned(R, Z, steps, order, mirrored, low_of, depth, far_rows, cuts, WEIGHTS):
        steps_of[op[0]](*op[1:])
    if 2 * depth != LANES:
        @pl.loop(0, blocks)
        def _(i):
            for c in range(len(cuts)):
                mirror_block(i, c)

    if far_rows != LANES:
        pl.loop(0, half)(place_far)

    for i in range(half + 1, blocks):
        rows = pl.ds(i * LANES, LANES)
        over = (i + half - blocks) * LANES
        cx[rows, :over] = cx[rows, n : n + over]

    for g in range(1, R):
        arrived(x0.at[:, columns_at(row_of(g))], ("field", g))
    for index in range(TERMS - 1):
        source = x0 if index == 0 else xs.at[(index + 1) % 2]
        target = xs.at[index % 2]
        scale = 1.0 / (TERMS - index)

        product = jnp.dot(source[...], cx[:, :n], preferred_element_type=jnp.float32)
        target[...] = (x0[...].astype(jnp.float32) + scale * product).astype(jnp.bfloat16)

    source, last = xs.at[TERMS % 2], xs.at[(TERMS - 1) % 2]
    pieces = max(1, row_rows // (2 * LANES))
    part_columns = row_rows // pieces
    for k in range(pieces):
        for g in reversed(range(R)):
            to, columns = row_of(g), pl.ds(k * part_columns, part_columns)
            there = pl.ds(pl.multiple_of(to * row_rows + k * part_columns, part_columns), part_columns)
            product = jnp.dot(source[...], cx[:, there], preferred_element_type=jnp.float32)
            value = (x0[:, there].astype(jnp.float32) + product).astype(jnp.bfloat16)
            if g:
                last[:, there] = value
                send(last.at[:, there], ot.at[slab_at(row), columns], (to, col), ("out", g, k), "out")
            else:
                out_ref[slab_at(row), columns] = value
    for k in range(pieces):
        for g in reversed(range(1, R)):
            source, columns = slab_at(row_of(g)), pl.ds(k * part_columns, part_columns)
            arrived(ot.at[source, columns], ("out", g, k))
            out_ref[source, columns] = ot[source, columns]
    for kind, (index, copies) in sends.items():
        if kind in ("field", "out"):
            sent = x0.at[:, : (R - 1) * row_rows]
        elif kind == "far_core":
            sent = f0
        elif kind == "far":
            sent = part.at[: copies * far_rows, :LANES]
        else:
            sent = part.at[: copies * depth, columns_of(kind[1])]
        pltpu.make_async_remote_copy(
            src_ref=sent, dst_ref=sent, send_sem=send_sem.at[index],
            recv_sem=recv_sem.at[0], device_id=partner, device_id_type=MESH).wait_send()


def on_device(R, Z, mode_profiles, region_labels, gain_table, index_table, field_in):
    points, n = mode_profiles.shape
    width = n // 2
    far_rows = n // (4 * Z)
    depth = n // (R * Z * 2)
    mine_cols = field_in.shape[1] // R
    steps = max(1, n // R // (2 * LANES))
    messages = SPLITS * (R * steps + R * Z + 2 * (R - 1) * Z) + (2 + max(1, n // R // (2 * LANES))) * (R - 1) + 1 + Z
    bf16 = jnp.bfloat16
    turned = pl.pallas_call(
        functools.partial(kernel, R, Z, n),
        out_shape=pltpu.VMEM(field_in.shape[::-1], bf16),
        in_specs=[
            pl.BlockSpec(memory_space=pl.ANY),
            pl.BlockSpec(memory_space=pl.ANY),
            pl.BlockSpec(memory_space=pl.ANY),
            pl.BlockSpec(memory_space=pl.ANY),
            pl.BlockSpec(memory_space=pl.ANY),
        ],
        out_specs=pl.BlockSpec(memory_space=pltpu.VMEM),
        scratch_shapes=[
            pltpu.VMEM((points, n), bf16),
            pltpu.VMEM((points // LANES, LANES), jnp.int32),
            pltpu.SMEM(gain_table.shape, jnp.float32),
            pltpu.SMEM(index_table.shape, jnp.float32),
            pltpu.VMEM(field_in.shape, bf16),
            pltpu.VMEM(field_in.shape[::-1], bf16),
            pltpu.VMEM((points, n + width - LANES), bf16),
            pltpu.VMEM((n, width), bf16),
            pltpu.VMEM((R * Z, depth, width), bf16),
            pltpu.VMEM(((R - 1) * Z, depth, width), bf16),
            pltpu.VMEM((Z, depth, width), bf16),
            pltpu.VMEM((n // 2, LANES), bf16),
            pltpu.VMEM((Z * far_rows, LANES), bf16),
            pltpu.VMEM((Z, far_rows, LANES), bf16),
            pltpu.VMEM((R, far_rows, LANES), bf16),
            pltpu.VMEM((n // 2, LANES), bf16),
            pltpu.VMEM((n, n + width - LANES), bf16),
            pltpu.VMEM((mine_cols, n), bf16),
            pltpu.VMEM((2, mine_cols, n), bf16),
            pltpu.VMEM(field_in.shape[::-1], bf16),
            pltpu.SemaphoreType.DMA((2 * SPLITS + 4,)),
            pltpu.SemaphoreType.DMA((messages,)),
            pltpu.SemaphoreType.DMA((SPLITS * Z,)),
            pltpu.SemaphoreType.DMA((SPLITS * Z,)),
            pltpu.SemaphoreType.DMA((2 * Z,)),
            pltpu.SemaphoreType.DMA((points // LANES,)),
            pltpu.SemaphoreType.DMA((4,)),
        ],
        compiler_params=pltpu.CompilerParams(
            collective_id=0, has_side_effects=True, vmem_limit_bytes=60 * 1024 * 1024),
    )(region_labels.reshape(-1, LANES), gain_table, index_table, mode_profiles, field_in)
    return turned.T


def solution(mesh):
    return jax.shard_map(
        functools.partial(on_device, mesh.shape["row"], mesh.shape["col"] // 2),
        mesh=mesh,
        in_specs=(P(("row", "col"), None), P(("row", "col")), P(), P(), P("row", "col")),
        out_specs=P("row", "col"),
        check_vma=False,
    )
```

```python
import functools

import jax
import jax.numpy as jnp
from jax import lax
from jax.experimental import pallas as pl
from jax.experimental.pallas import tpu as pltpu
from jax.sharding import PartitionSpec as P

TERMS = 6
LANES = 128
MESH = pl.DeviceIdType.MESH


def lowest_bit(g):
    t = 0
    while not (g >> t) & 1:
        t += 1
    return t


TILES = (2, 2, 2, 2)
SPLITS = len(TILES)
WEIGHTS = dict(
    link=102069.93, routed=2.35, extra=0.5, near=1.15, lag=0,
    reduce=2.45, reduce_cut=1.25, reduce_step=0.32, reduce_low=-0.6,
    forward=-0.89, forward_cut=-0.13, forward_far=-1.52, forward_low=-0.8,
    product=3.1, product_cut=0.92, block=4.26, block_cut=0.1,
    far_product=2.46, far_core=2.56, far_row=2.18, far_own=3.07, far_forward=1.94, far_block=2.99)


def cuts_of(width):
    edges = [width // LANES * sum(TILES[:c]) // sum(TILES) * LANES for c in range(SPLITS + 1)]
    return [(first, after - first) for first, after in zip(edges, edges[1:])]


def nearest(z, p, Z):
    edge, away = min(z, Z - 1 - z), 1 - 2 * (2 * z // Z)
    if p > 2 * edge:
        return z + away * (p - edge)
    return z + (away * (p // 2) if p % 2 == 0 else -away * ((p + 1) // 2))


def planned(R, Z, steps, order, mirrored, low_of, depth, far_rows, cuts, w):
    per_step = Z // steps
    final = (steps - 1, 0, per_step - 1)
    ops = []
    for c in range(len(cuts)):
        ops += [("product", c, p, g) for p in range(steps) for g in order]
        ops += [("reduce", c, p, g, e) for p in range(steps) for g in order for e in range(per_step)]
        ops += [("forward", c, g, p) for p in range(Z) for g in range(R)]
        ops += [("block", c, g, p) for p in range(Z) for g in range(R)]
    ops += [("far_product", 0), ("far_core", 0), ("far_row", 0), ("far_own", 0)]
    ops += [("far_forward", p) for p in range(1, Z)] + [("far_block", p) for p in range(Z)]
    at, free, start = {}, {}, 3.6

    def needs(op):
        kind, c = op[:2]
        if kind in ("product", "far_product"):
            return []
        if kind.startswith("far"):
            return {
                "far_core": [("far_core_in",)], "far_row": [("far_z_in",)], "far_own": [("far_row_in",)],
                "far_forward": [("far_spread", c), ("far_own", 0)], "far_block": [("far_partner", c), ("far_forward" if c else "far_own", c)],
            }[kind]
        if kind == "reduce":
            p, g, e = op[2:]
            j = p * per_step + e
            keys = [("product", c, p, g), ("core", c, g, j)] + [("row", c, t, g, j) for t in range(low_of(g))]
            return keys + ([("sums", c, i) for i in range(Z - 1)] if (p, g, e) == final else [])
        g, p = op[2:]
        if kind == "block":
            return [("forward", c, g, p), ("spread_core", c, g, p)]
        return [("spread", c, g, p) if (g or p) else ("reduce", c, *final)]

    def rank(op):
        kind, c = op[:2]
        if kind == "reduce":
            p, g, e = op[2:]
            return w["reduce"] + w["reduce_cut"] * c + w["reduce_step"] * p + w["reduce_low"] * low_of(g) + 0.01 * e - 0.001 * g
        if kind == "forward":
            return w["forward"] + w["forward_cut"] * c + w["forward_far"] * op[3] - w["forward_low"] * low_of(op[2])
        return w[kind] + (0.001 if kind.startswith("far") else w[kind + "_cut"]) * c

    def sent(now, link, amount, key):
        free[link] = max(free.get(link, start), now) + amount
        at[key] = free[link] + (w["near"] if link == "core" else w["routed"])

    def sent_along(now, amount, z, goal):
        way, end = (1 if goal > z else -1), now
        for k in range(z, goal, way):
            free[k, way] = max(free.get((k, way), start), now) + 2 * amount
            end = max(end, free[k, way])
        return end + w["routed"] + w["extra"] * (abs(goal - z) - 1)

    def sent_near(now, amount, key):
        ends = {(z, nearest(z, p, Z)): sent_along(now, amount, z, nearest(z, p, Z)) for p in range(1, Z) for z in range(Z)}
        for p in range(1, Z):
            at[(*key, p)] = max(ends[nearest(z, p, Z), z] for z in range(Z))

    def goal_of(z, p, e):
        return (z // per_step + 1 + p) % steps * per_step + (z % per_step + 1 + e) % per_step

    wanted, ranks = {op: needs(op) for op in ops}, {op: rank(op) for op in ops}
    now, left, done = start, list(ops), []
    far = far_rows * LANES * 2 / w["link"]
    while left:
        ripe, later = None, None
        for op in left:
            ready = 0.0
            for key in wanted[op]:
                ready = max(ready, at.get(key, 1e9))
            if op[0] in ("reduce", "forward"):
                ready += w["lag"]
            if ready <= now:
                ripe = min(ripe or (ranks[op], op), (ranks[op], op))
            elif ready < 1e9 and not ripe:
                later = min(later or (ready, ranks[op], op), (ready, ranks[op], op))
        op = ripe[1] if ripe else later[2]
        now = now if ripe else later[0]
        left.remove(op)
        done.append(op)
        kind, c = op[:2]
        tiles = cuts[c][1] / LANES if not kind.startswith("far") else 0
        strip = depth * tiles * LANES * 2 / w["link"]
        if kind == "far_product":
            now += 0.8
            sent(now, "core", far * Z / 7, ("far_core_in",))
        elif kind == "far_core":
            now += 0.1
            at["far_z_in",] = max(sent_along(now, far, z, (z + k) % Z) for k in range(1, Z) for z in range(Z))
        elif kind == "far_row":
            now += 0.1
            sent(now, "row", far * 4 / 3 * (R - 1), ("far_row_in",))
        elif kind == "far_own":
            now += 0.1
            sent_near(now, far, ("far_spread",))
            sent(now, "core", far / 7, ("far_partner", 0))
        elif kind == "far_forward":
            now += 0.05
            sent(now, "core", far / 7, ("far_partner", c))
        elif kind == "far_block":
            now += 0.2
        elif kind == "product":
            p, g = op[2:]
            now += tiles * 0.11 + 0.15
            for e in range(per_step):
                sent(now, "core", strip / 7, ("core", c, mirrored(g), p * per_step + e))
        elif kind == "reduce":
            p, g, e = op[2:]
            now += tiles * 0.025 + 0.03
            if g:
                low = low_of(g)
                sent(now, "row", strip, ("row", c, low, g ^ (1 << low), p * per_step + e))
            elif (p, g, e) != final:
                at["sums", c, p * per_step + e] = max(sent_along(now, strip, z, goal_of(z, p, e)) for z in range(Z))
        elif kind == "forward":
            g, p = op[2:]
            now += 0.08
            if g == 0 and p == 0:
                sent_near(now, strip, ("spread", c, 0))
            direct = c == len(cuts) - 1 and p == Z - 1
            for there in reached_from(g, p, direct, R, low_of):
                sent(now, "row", strip * (4 / 3 if direct else 1), ("spread", c, there, p))
            sent(now, "core", strip / 7, ("spread_core", c, mirrored(g), p))
        else:
            now += tiles * 0.075
        at[op] = now
    return done


def reached_from(g, p, direct, R, low_of):
    if direct:
        return list(reversed(range(1, R))) if g == 0 else []
    return [g | (1 << t) for t in reversed(range(low_of(g)))]


def kernel(R, Z, n, labels_hbm, gain_hbm, index_hbm, p_hbm, f_hbm, out_ref, p_ref, labels_ref, gain_ref, index_ref, f_ref, ft, s2, part, r0, rt, rz, far, f0, fz, fr, fg, cx, x0, xs, ot, send_sem, recv_sem, z_sem, spread_sem, far_sem, load_sem, small_sem):
    bits = R.bit_length() - 1
    blocks = n // LANES
    half = blocks // 2
    width = half * LANES
    depth = n // (R * Z * 2)
    far_rows = n // (4 * Z)
    mine_cols = x0.shape[0]
    row_rows = n // R
    step_rows = min(2 * LANES, row_rows)
    steps = row_rows // step_rows
    per_step = Z // steps
    row, col = lax.axis_index("row"), lax.axis_index("col")
    z, h = col // 2, col % 2
    partner = (row, z * 2 + 1 - h)

    def flip(r, t):
        mask0, mask1 = 1 << t, 1 << (bits - 1 - t)
        mask = mask0 + h * (mask1 - mask0)
        return r + mask * (1 - 2 * ((r // mask) % 2))

    def row_of(g):
        r = row
        for t in range(bits):
            if (g >> t) & 1:
                r = flip(r, t)
        return r

    def mirrored(g):
        return sum(((g >> t) & 1) << (bits - 1 - t) for t in range(bits))

    def low_of(g):
        return lowest_bit(g) if g else bits

    def group_of(p):
        return (z // per_step + 1 + p) % steps

    def z_of(p, e):
        return group_of(p) * per_step + (z % per_step + 1 + e) % per_step

    def near(p):
        if p == 0:
            return z
        edge = jnp.minimum(z, Z - 1 - z)
        away = 1 - 2 * (2 * z // Z)
        both_sides = away * (p // 2) if p % 2 == 0 else -away * ((p + 1) // 2)
        return z + jnp.where(p <= 2 * edge, both_sides, away * (p - edge))

    def strip_of(r, zz, hh):
        return (r * Z + zz) * 2 + hh

    cuts = cuts_of(width)

    def columns_of(c):
        return pl.ds(*cuts[c])

    def rows_of(ref, s, c):
        return ref.at[pl.ds(pl.multiple_of(s * depth, depth), depth), columns_of(c)]

    def window_of(s, c):
        first, size = cuts[c]
        start = pl.multiple_of((s * depth // LANES) * LANES + first, LANES)
        return cx.at[pl.ds(pl.multiple_of(s * depth, depth), depth), pl.ds(start, size)]

    ids, sends = {}, {}

    def slot(key):
        return recv_sem.at[ids.setdefault(key, len(ids))]

    def send_to(src, dst, device, sem, kind):
        index, copies = sends.get(kind, (len(sends), 0))
        sends[kind] = index, copies + 1
        pltpu.make_async_remote_copy(
            src_ref=src, dst_ref=dst, send_sem=send_sem.at[index],
            recv_sem=sem, device_id=device, device_id_type=MESH).start()

    def send(src, dst, device, key, kind):
        send_to(src, dst, device, slot(key), kind)

    def arrived_at(ref, sem):
        pltpu.make_async_remote_copy(
            src_ref=ref, dst_ref=ref, send_sem=send_sem.at[0],
            recv_sem=sem, device_id=partner, device_id_type=MESH).wait_recv()

    def arrived(ref, key):
        arrived_at(ref, slot(key))

    rows_at_once = LANES
    loads = p_ref.shape[0] // rows_at_once

    def load(i):
        rows = pl.ds(i * rows_at_once, rows_at_once)
        return pltpu.make_async_copy(p_hbm.at[rows, :], p_ref.at[rows, :], load_sem.at[i])

    load_field = pltpu.make_async_copy(f_hbm, f_ref, small_sem.at[0])
    small = [(labels_hbm, labels_ref), (gain_hbm, gain_ref), (index_hbm, index_ref)]
    small = [pltpu.make_async_copy(here, there, small_sem.at[1 + k]) for k, (here, there) in enumerate(small)]
    for copy in small:
        copy.start()
    load(0).start()
    load_field.start()
    for i in range(1, loads):
        load(i).start()

    barrier = pltpu.get_barrier_semaphore()
    peers = [(row_of(g), col) for g in range(1, R)]
    peers += [(row, ((z + k) % Z) * 2 + h) for k in range(1, Z)] + [partner]
    for peer in peers:
        pl.semaphore_signal(barrier, inc=1, device_id=peer, device_id_type=MESH)

    def columns_at(r):
        return pl.ds(pl.multiple_of(r * row_rows, row_rows), row_rows)

    def slab_at(r):
        return pl.ds(pl.multiple_of(r * mine_cols, mine_cols), mine_cols)

    for copy in small:
        copy.wait()
    labels = labels_ref[...]
    weight = jnp.zeros(labels.shape, jnp.float32)
    for region in range(gain_ref.shape[0]):
        weight = jnp.where(labels == region, gain_ref[region] + index_ref[region], weight)
    for i in range(loads):
        rows = pl.ds(i * rows_at_once, rows_at_once)
        along = jnp.broadcast_to(weight[i : i + 1, :], (LANES, LANES)).T
        load(i).wait()
        for c in range(n // LANES):
            columns = pl.ds(c * LANES, LANES)
            scaled = (p_ref[rows, columns].astype(jnp.float32) * along).astype(jnp.bfloat16)
            s2[rows, columns] = scaled
            if c * LANES < width - LANES:
                s2[rows, pl.ds(n + c * LANES, LANES)] = scaled
        if i == loads // 2:
            load_field.wait()
            ft[...] = f_ref[...].T

    pl.semaphore_wait(barrier, len(peers))
    for g in range(1, R):
        to = row_of(g)
        send(ft.at[slab_at(to), :], x0.at[:, columns_at(row)], (to, col), ("field", g), "field")
    x0[:, columns_at(row)] = ft[slab_at(row), :]

    order = sorted(range(R), key=lambda g: (low_of(g), -g))
    stage_slot = {}
    for t in range(bits):
        for g in range(R):
            if g % (2 << t) == 0:
                stage_slot[t, g] = len(stage_slot)

    met = set()

    def reduce(c, p, g, e):
        low, j = low_of(g), p * per_step + e
        zz, columns = z_of(p, e), columns_of(c)
        if (c, p, g) not in met:
            met.add((c, p, g))
            arrived(r0.at[g * Z + p * per_step : g * Z + (p + 1) * per_step, :, columns], ("core", c, g, p))
        own = rows_of(part, strip_of(row_of(g), zz, h), c)
        total = own[...].astype(jnp.float32) + r0[g * Z + j, :, columns].astype(jnp.float32)
        for t in range(low):
            piece = rt.at[stage_slot[t, g] * Z + j, :, columns]
            arrived(piece, ("row", c, t, g, j))
            total = total + piece[...].astype(jnp.float32)
        if g:
            own[...] = total.astype(jnp.bfloat16)
            seen = g ^ (1 << low)
            send(own, rt.at[stage_slot[low, seen] * Z + j, :, columns], (flip(row, low), col), ("row", c, low, seen, j), ("sum", c))
        elif j < Z - 1:
            own[...] = total.astype(jnp.bfloat16)
            send_to(own, rz.at[z, :, columns], (row, zz * 2 + h), z_sem.at[c], ("sum", c))
        else:
            arrived_at(rz.at[1:, :, columns], z_sem.at[c])
            for i in range(1, Z):
                source = (z + i) % Z
                total = total + rz[source, :, columns].astype(jnp.float32)
            window_of(strip_of(row, z, h), c)[...] = total.astype(jnp.bfloat16)

    def product(c, p, g):
        first, size = cuts[c]
        r, q = row_of(g), group_of(p)
        base = pl.multiple_of(r * row_rows + q * step_rows, step_rows)
        left = p_ref[:, pl.ds(base, step_rows)].T
        right = s2[:, pl.ds(pl.multiple_of(base + first, LANES), size + step_rows - LANES)]
        both = jnp.dot(left, right, preferred_element_type=jnp.float32)
        for k in range(step_rows // LANES):
            piece = both[k * LANES : (k + 1) * LANES, k * LANES : k * LANES + size]
            part[pl.ds(base + k * LANES, LANES), columns_of(c)] = piece.astype(jnp.bfloat16)
        for e in range(per_step):
            j = p * per_step + e
            there = r0.at[mirrored(g) * Z + j, :, columns_of(c)]
            send(rows_of(part, strip_of(r, z_of(p, e), 1 - h), c), there, partner, ("core", c, mirrored(g), p), ("sum", c))

    def mirror_block(i, c):
        rows = pl.ds(pl.multiple_of(i * LANES, LANES), LANES)
        first, size = cuts[c]
        for d in range(max(1, first // LANES), min(half, (first + size) // LANES)):
            to = pl.multiple_of(((i + d) % blocks) * LANES, LANES)
            block = cx[rows, pl.ds(pl.multiple_of((i + d) * LANES, LANES), LANES)]
            cx[pl.ds(to, LANES), rows] = block.T

    def forward(c, g, p):
        view = window_of(strip_of(row_of(g), near(p), h), c)
        if g:
            arrived(view, ("spread", c, g, p))
        elif p:
            arrived_at(view, spread_sem.at[c * Z + near(p)])
        else:
            for k in range(1, Z):
                send_to(view, view, (row, near(k) * 2 + h), spread_sem.at[c * Z + z], ("spread", c))
        for there in reached_from(g, p, c == len(cuts) - 1 and p == Z - 1, R, low_of):
            send(view, view, (row_of(there - g), col), ("spread", c, there, p), ("spread", c))
        send(view, view, partner, ("spread_core", c, mirrored(g), p), ("spread", c))

    def block(c, g, p):
        arrived(window_of(strip_of(row_of(g), near(p), 1 - h), c), ("spread_core", c, g, p))
        if 2 * depth == LANES:
            mirror_block(row_of(g) * Z + near(p), c)

    def far_at(hh, zz, count=1):
        return pl.ds(pl.multiple_of((hh * Z + zz) * far_rows, far_rows), count * far_rows)

    def far_product(_):
        for hh in (1 - h, h):
            for k in range(half // 2):
                base = pl.multiple_of((hh * (half // 2) + k) * LANES, LANES)
                left = p_ref[:, pl.ds(base, LANES)].T
                right = s2[:, pl.ds(pl.multiple_of(base + half * LANES, LANES), LANES)]
                far[pl.ds(base, LANES), :] = jnp.dot(left, right, preferred_element_type=jnp.float32).astype(jnp.bfloat16)
        send(far.at[far_at(1 - h, 0, Z), :], f0, partner, ("far_core",), "far_core")

    def far_core(_):
        arrived(f0, ("far_core",))
        rows = far_at(h, 0, Z)
        far[rows, :] = (far[rows, :].astype(jnp.float32) + f0[...].astype(jnp.float32)).astype(jnp.bfloat16)
        for k in range(1, Z):
            zz = (z + k) % Z
            send_to(far.at[far_at(h, zz), :], fz.at[z], (row, zz * 2 + h), far_sem.at[Z], "far")

    def far_row(_):
        rows = far_at(h, z)
        total = far[rows, :].astype(jnp.float32)
        arrived_at(fz.at[1:], far_sem.at[Z])
        for k in range(1, Z):
            source = (z + k) % Z
            total = total + fz[source].astype(jnp.float32)
        far[rows, :] = total.astype(jnp.bfloat16)
        for g in reversed(range(1, R)):
            send(far.at[rows, :], fr.at[g], (row_of(g), col), ("far_row", g), "far")

    def far_own(_):
        rows = far_at(h, z)
        total = far[rows, :].astype(jnp.float32)
        for g in range(1, R):
            arrived(fr.at[g], ("far_row", g))
            total = total + fr[g].astype(jnp.float32)
        fg[rows, :] = total.astype(jnp.bfloat16)
        view = fg.at[rows, :]
        for k in range(1, Z):
            send_to(view, view, (row, near(k) * 2 + h), far_sem.at[z], "far")
        send(view, view, partner, ("far_partner", 0), "far")

    def far_forward(p):
        view = fg.at[far_at(h, near(p)), :]
        arrived_at(view, far_sem.at[near(p)])
        send(view, view, partner, ("far_partner", p), "far")

    def place_far(i):
        here, there = pl.multiple_of(i * LANES, LANES), pl.multiple_of((i + half) * LANES, LANES)
        piece = fg[pl.ds(here, LANES), :]
        cx[pl.ds(here, LANES), pl.ds(there, LANES)] = piece
        cx[pl.ds(there, LANES), pl.ds(here, LANES)] = piece.T

    def far_block(p):
        arrived(fg.at[far_at(1 - h, near(p)), :], ("far_partner", p))
        if far_rows == LANES:
            for hh in range(2):
                place_far(hh * Z + near(p))

    steps_of = {"far_product": far_product, "far_core": far_core, "far_row": far_row, "far_own": far_own}
    steps_of |= {"far_forward": far_forward, "far_block": far_block}
    steps_of |= {"product": product, "reduce": reduce, "forward": forward, "block": block}
    for op in planned(R, Z, steps, order, mirrored, low_of, depth, far_rows, cuts, WEIGHTS):
        steps_of[op[0]](*op[1:])
    if 2 * depth != LANES:
        @pl.loop(0, blocks)
        def _(i):
            for c in range(len(cuts)):
                mirror_block(i, c)

    if far_rows != LANES:
        pl.loop(0, half)(place_far)

    for i in range(half + 1, blocks):
        rows = pl.ds(i * LANES, LANES)
        over = (i + half - blocks) * LANES
        cx[rows, :over] = cx[rows, n : n + over]

    for g in range(1, R):
        arrived(x0.at[:, columns_at(row_of(g))], ("field", g))
    for index in range(TERMS - 1):
        source = x0 if index == 0 else xs.at[(index + 1) % 2]
        target = xs.at[index % 2]
        scale = 1.0 / (TERMS - index)

        product = jnp.dot(source[...], cx[:, :n], preferred_element_type=jnp.float32)
        target[...] = (x0[...].astype(jnp.float32) + scale * product).astype(jnp.bfloat16)

    source, last = xs.at[TERMS % 2], xs.at[(TERMS - 1) % 2]
    pieces = max(1, row_rows // (2 * LANES))
    part_columns = row_rows // pieces
    for k in range(pieces):
        for g in reversed(range(R)):
            to, columns = row_of(g), pl.ds(k * part_columns, part_columns)
            there = pl.ds(pl.multiple_of(to * row_rows + k * part_columns, part_columns), part_columns)
            product = jnp.dot(source[...], cx[:, there], preferred_element_type=jnp.float32)
            value = (x0[:, there].astype(jnp.float32) + product).astype(jnp.bfloat16)
            if g:
                last[:, there] = value
                send(last.at[:, there], ot.at[slab_at(row), columns], (to, col), ("out", g, k), "out")
            else:
                out_ref[slab_at(row), columns] = value
    for k in range(pieces):
        for g in reversed(range(1, R)):
            source, columns = slab_at(row_of(g)), pl.ds(k * part_columns, part_columns)
            arrived(ot.at[source, columns], ("out", g, k))
            out_ref[source, columns] = ot[source, columns]
    for kind, (index, copies) in sends.items():
        if kind in ("field", "out"):
            sent = x0.at[:, : (R - 1) * row_rows]
        elif kind == "far_core":
            sent = f0
        elif kind == "far":
            sent = part.at[: copies * far_rows, :LANES]
        else:
            sent = part.at[: copies * depth, columns_of(kind[1])]
        pltpu.make_async_remote_copy(
            src_ref=sent, dst_ref=sent, send_sem=send_sem.at[index],
            recv_sem=recv_sem.at[0], device_id=partner, device_id_type=MESH).wait_send()


def on_device(R, Z, mode_profiles, region_labels, gain_table, index_table, field_in):
    points, n = mode_profiles.shape
    width = n // 2
    far_rows = n // (4 * Z)
    depth = n // (R * Z * 2)
    mine_cols = field_in.shape[1] // R
    steps = max(1, n // R // (2 * LANES))
    messages = SPLITS * (R * steps + R * Z + 2 * (R - 1) * Z) + (2 + max(1, n // R // (2 * LANES))) * (R - 1) + 1 + Z
    bf16 = jnp.bfloat16
    turned = pl.pallas_call(
        functools.partial(kernel, R, Z, n),
        out_shape=pltpu.VMEM(field_in.shape[::-1], bf16),
        in_specs=[
            pl.BlockSpec(memory_space=pl.ANY),
            pl.BlockSpec(memory_space=pl.ANY),
            pl.BlockSpec(memory_space=pl.ANY),
            pl.BlockSpec(memory_space=pl.ANY),
            pl.BlockSpec(memory_space=pl.ANY),
        ],
        out_specs=pl.BlockSpec(memory_space=pltpu.VMEM),
        scratch_shapes=[
            pltpu.VMEM((points, n), bf16),
            pltpu.VMEM((points // LANES, LANES), jnp.int32),
            pltpu.SMEM(gain_table.shape, jnp.float32),
            pltpu.SMEM(index_table.shape, jnp.float32),
            pltpu.VMEM(field_in.shape, bf16),
            pltpu.VMEM(field_in.shape[::-1], bf16),
            pltpu.VMEM((points, n + width - LANES), bf16),
            pltpu.VMEM((n, width), bf16),
            pltpu.VMEM((R * Z, depth, width), bf16),
            pltpu.VMEM(((R - 1) * Z, depth, width), bf16),
            pltpu.VMEM((Z, depth, width), bf16),
            pltpu.VMEM((n // 2, LANES), bf16),
            pltpu.VMEM((Z * far_rows, LANES), bf16),
            pltpu.VMEM((Z, far_rows, LANES), bf16),
            pltpu.VMEM((R, far_rows, LANES), bf16),
            pltpu.VMEM((n // 2, LANES), bf16),
            pltpu.VMEM((n, n + width - LANES), bf16),
            pltpu.VMEM((mine_cols, n), bf16),
            pltpu.VMEM((2, mine_cols, n), bf16),
            pltpu.VMEM(field_in.shape[::-1], bf16),
            pltpu.SemaphoreType.DMA((2 * SPLITS + 4,)),
            pltpu.SemaphoreType.DMA((messages,)),
            pltpu.SemaphoreType.DMA((SPLITS,)),
            pltpu.SemaphoreType.DMA((SPLITS * Z,)),
            pltpu.SemaphoreType.DMA((Z + 1,)),
            pltpu.SemaphoreType.DMA((points // LANES,)),
            pltpu.SemaphoreType.DMA((4,)),
        ],
        compiler_params=pltpu.CompilerParams(
            collective_id=0, has_side_effects=True, vmem_limit_bytes=60 * 1024 * 1024),
    )(region_labels.reshape(-1, LANES), gain_table, index_table, mode_profiles, field_in)
    return turned.T


def solution(mesh):
    return jax.shard_map(
        functools.partial(on_device, mesh.shape["row"], mesh.shape["col"] // 2),
        mesh=mesh,
        in_specs=(P(("row", "col"), None), P(("row", "col")), P(), P(), P("row", "col")),
        out_specs=P("row", "col"),
        check_vma=False,
    )
```
